32 devices in a mesh: replica: 16 (over z, x, core), fsdp: 2 (over y).
Axes of the slice: x: 2, y: 2, z: 4, core: 2. Of those that a mesh axis runs over, the one named last changes fastest.
Arguments:
- block_in: bfloat16 [4096, 1024], P(('replica', 'fsdp')), may hold values from -6 to 6
- w_query: bfloat16 [1024, 2048], P('fsdp'), may hold values from -1 to 1
- key_projection: bfloat16 [1024, 1024], P('fsdp'), may hold values from -1 to 1
- value_projection: bfloat16 [1024, 1024], P('fsdp'), may hold values from -0.1875 to 0.1875
- w_out: bfloat16 [2048, 1024], P('fsdp'), may hold values from -0.5 to 0.5
- w_gate: bfloat16 [1024, 3072], P('fsdp'), may hold values from -0.1875 to 0.1875
- w_up: bfloat16 [1024, 3072], P('fsdp'), may hold values from -0.1875 to 0.1875
- w_down: bfloat16 [3072, 1024], P('fsdp'), may hold values from -0.109375 to 0.109375
- attn_gain: float32 [1024], replicated, may hold values from 0.5 to 1.5
- mlp_gain: float32 [1024], replicated, may hold values from 0.5 to 1.5
- query_gain: float32 [128], replicated, may hold values from 0.5 to 3.5
- key_norm_gain: float32 [128], replicated, may hold values from 0.5 to 3.5
- segment_ids: int32 [16, 256], P('replica'), may hold values from 0 to 2, as said below
- positions: int32 [4096], P(('replica', 'fsdp')), may hold values from 0 to 255, as said below
- cotangent: bfloat16 [4096, 1024], P(('replica', 'fsdp')), may hold values from -6 to 6
Outputs:
- block_out: bfloat16 [4096, 1024], P(('replica', 'fsdp'))
- d_block_in: float32 [4096, 1024], P(('replica', 'fsdp'))
- grad_query: float32 [1024, 2048], P('fsdp')
- grad_key: float32 [1024, 1024], P('fsdp')
- grad_value: float32 [1024, 1024], P('fsdp')
- grad_out: float32 [2048, 1024], P('fsdp')
- grad_gate: float32 [1024, 3072], P('fsdp')
- grad_up: float32 [1024, 3072], P('fsdp')
- grad_down: float32 [3072, 1024], P('fsdp')
- grad_attn_gain: float32 [1024], replicated
- grad_mlp_gain: float32 [1024], replicated
- grad_query_gain: float32 [128], replicated
- grad_key_gain: float32 [128], replicated
The draws below stay inside these ranges and needn't reach their ends.
Inputs may be any that keep to these rules, and one draw needn't show every extreme that they name: `segment_ids`: in each sequence the document numbers start at 0 at its first token and rise by one at each new document, never falling; a sequence holds at most three documents, the first sequence a single one, every other sequence exactly three. `positions`: A token's position is its place within its document, counted from 0 at the document's first token.
All inputs are finite; a program needn't handle non-finite values.
Results may differ from the reference program's by a relative error of at most 0.02.
The reference program's roundings to bfloat16 on the way count: a program that leaves them out, or rounds other values in their place, can miss the bound.
Values may be sent and summed in bfloat16 or wider, within the bound.
No kernel may reach another device: no remote copies, remote signals or barrier semaphores. Data moves between devices by JAX's collectives and lax.ppermute only.
A program may use at most 192 MiB of HBM per device.

```python
import jax
import jax.numpy as jnp
from jax import lax

MODEL_WIDTH = 1024
QUERY_HEADS = 16
KEY_VALUE_HEADS = 8
HEAD_SIZE = 128
FF = 3072
TOK_DEV = 128
LEN = 256
NSEQ = 16
TOKENS = 4096


def document_layout(key):
    column = jnp.arange(LEN, dtype=jnp.int32)[None, :]
    half = LEN // 2
    first = jax.random.randint(jax.random.fold_in(key, 11), (NSEQ, 1), 1, half + 1).astype(jnp.int32)
    second = jax.random.randint(jax.random.fold_in(key, 13), (NSEQ, 1), half + 1, LEN).astype(jnp.int32)
    row = jnp.arange(NSEQ, dtype=jnp.int32)[:, None]
    first = jnp.where(row == 0, LEN, first).astype(jnp.int32)
    second = jnp.where(row == 0, LEN, second).astype(jnp.int32)
    past_first = (column >= first).astype(jnp.int32)
    past_second = (column >= second).astype(jnp.int32)
    segments = (past_first + past_second).astype(jnp.int32)
    begin = jnp.where(past_second == 1, second, jnp.where(past_first == 1, first, 0)).astype(jnp.int32)
    return (segments, (column - begin).astype(jnp.int32))


def draw_segment_ids(key, part):
    return document_layout(key)[0]


def draw_positions(key, part):
    return document_layout(key)[1].reshape(TOKENS)


def draw_block_in(key, part):
    rows = jnp.clip(jax.random.normal(jax.random.fold_in(key, 31), (TOKENS, MODEL_WIDTH), jnp.float32), -6.0, 6.0)
    return rows.astype(jnp.bfloat16)


def attention_pair(key):
    scale = MODEL_WIDTH ** (-0.5)
    query_rest = jnp.clip(jax.random.normal(jax.random.fold_in(key, 22), (MODEL_WIDTH, QUERY_HEADS * HEAD_SIZE), jnp.float32), -4.0, 4.0)
    key_remainder = jnp.clip(jax.random.normal(jax.random.fold_in(key, 23), (MODEL_WIDTH, KEY_VALUE_HEADS * HEAD_SIZE), jnp.float32), -4.0, 4.0)
    query_full = query_rest
    key_full = key_remainder
    return (query_full * scale, key_full * scale)


def draw_w_query(key, part):
    return attention_pair(key)[0].astype(jnp.bfloat16)


def draw_key_projection(key, part):
    return attention_pair(key)[1].astype(jnp.bfloat16)


def gain_draw(key, salt):
    folded = jax.random.fold_in(key, salt)
    return jnp.exp(jax.random.uniform(folded, (HEAD_SIZE,), jnp.float32, jnp.log(0.5), jnp.log(3.5)))


def draw_query_gain(key, part):
    return gain_draw(key, 41)


def draw_key_norm_gain(key, part):
    return gain_draw(key, 42)


def with_spikes(result, key, source, target, parts, factor):
    def block_of(position):
        return (jnp.arange(result.shape[position]) // (result.shape[position] // parts)).reshape((-1,) + (1,) * (result.ndim - 1 - position))

    first = jax.random.permutation(key, parts)[block_of(target)]
    far = (block_of(target) + parts // 2) % parts
    return jnp.where((block_of(source) == first) | (block_of(source) == far), factor * result, result)


def levels(own_key, dims, cuts, smallest, top_value):
    level = 1.0
    for position, shards_of in cuts:
        steps = jax.random.uniform(jax.random.fold_in(jax.random.fold_in(own_key, 6), position), (shards_of,), jnp.float32, smallest / len(cuts), top_value / len(cuts))
        level = level * jnp.repeat(jnp.exp(steps), dims[position] // shards_of).reshape((-1,) + (1,) * (len(dims) - 1 - position))
    return level


def centred(own_key, shape, scale, limit, cuts=(), held_as=jnp.bfloat16):
    result = scale * jax.random.normal(own_key, shape, jnp.float32)
    if cuts:
        result = result * levels(own_key, shape, cuts, -0.22, 0.18)
    return jnp.clip(result, -limit, limit).astype(held_as)


def heavy_noise(stream_key, dims, scale, most, pieces, heavy, held_as=jnp.bfloat16):
    drawn = scale * jax.random.normal(stream_key, dims, jnp.float32)
    if pieces:
        drawn = drawn * levels(stream_key, dims, pieces, -0.22, 0.18)
    return jnp.clip(with_spikes(drawn, jax.random.fold_in(stream_key, 3), *heavy), -most, most).astype(held_as)


def setup_inputs(seed: int = 0) -> dict:
    streams_of = jax.random.split(jax.random.key(seed), 16)
    block_in = draw_block_in(jax.random.fold_in(streams_of[15], 71), 0)
    w_query = draw_w_query(jax.random.fold_in(streams_of[15], 71), 0)
    key_projection = draw_key_projection(jax.random.fold_in(streams_of[15], 71), 0)
    value_projection = centred(streams_of[3], (MODEL_WIDTH, KEY_VALUE_HEADS * HEAD_SIZE), MODEL_WIDTH ** -0.5, 0.1875, ((0, 2),))
    w_out = centred(streams_of[4], (QUERY_HEADS * HEAD_SIZE, MODEL_WIDTH), (QUERY_HEADS * HEAD_SIZE // 16) ** -0.5, 0.5, ((0, 2),))
    w_gate = centred(streams_of[5], (MODEL_WIDTH, FF), MODEL_WIDTH ** -0.5, 0.1875, ((0, 2),))
    w_up = centred(streams_of[6], (MODEL_WIDTH, FF), MODEL_WIDTH ** -0.5, 0.1875, ((0, 2),))
    w_down = centred(streams_of[7], (FF, MODEL_WIDTH), FF ** -0.5, 0.109375, ((0, 2),))
    attn_gain = jnp.clip(1.0 + 0.1 * jax.random.normal(streams_of[8], (MODEL_WIDTH,), jnp.float32), 0.5, 1.5)
    mlp_gain = jnp.clip(1.0 + 0.1 * jax.random.normal(streams_of[9], (MODEL_WIDTH,), jnp.float32), 0.5, 1.5)
    query_gain = draw_query_gain(jax.random.fold_in(streams_of[15], 71), 0)
    key_norm_gain = draw_key_norm_gain(jax.random.fold_in(streams_of[15], 71), 0)
    segment_ids = draw_segment_ids(jax.random.fold_in(streams_of[15], 71), 0)
    positions = draw_positions(jax.random.fold_in(streams_of[15], 71), 0)
    cotangent = heavy_noise(streams_of[14], (TOKENS, MODEL_WIDTH), 1.0, 6.0, ((0, 32),), (0, 1, 32, 2.75))
    return dict(block_in=block_in, w_query=w_query, key_projection=key_projection, value_projection=value_projection, w_out=w_out, w_gate=w_gate, w_up=w_up, w_down=w_down, attn_gain=attn_gain, mlp_gain=mlp_gain, query_gain=query_gain, key_norm_gain=key_norm_gain, segment_ids=segment_ids, positions=positions, cotangent=cotangent)


EPS = 1e-06
THETA = 1000000.0
NEG = -1e+30

def inv_rms(value):
    return lax.rsqrt(lax.optimization_barrier(jnp.mean(value * value, axis=-1, keepdims=True)) + EPS)

def norm_backward(grad, value, scale, gain):
    upstream = grad * gain
    return scale * (upstream - value * scale * scale * lax.optimization_barrier(jnp.mean(upstream * value, axis=-1, keepdims=True)))

def rope_tables(position_row, width):
    half = width // 2
    freq = jnp.exp(-(jnp.arange(half, dtype=jnp.float32) * (2.0 / width)) * jnp.log(jnp.float32(THETA)))
    angle = position_row.astype(jnp.float32)[:, None] * freq[None, :]
    cos_tab = jnp.concatenate([jnp.cos(angle), jnp.cos(angle)], axis=-1)[:, None, :]
    sin_tab = jnp.concatenate([jnp.sin(angle), jnp.sin(angle)], axis=-1)[:, None, :]
    return (cos_tab, sin_tab)

def rotate(values_in):
    half = values_in.shape[-1] // 2
    return jnp.concatenate([-values_in[..., half:], values_in[..., :half]], axis=-1)

def rotate_back(values_in):
    half = values_in.shape[-1] // 2
    return jnp.concatenate([values_in[..., half:], -values_in[..., :half]], axis=-1)

def kept_bfloat16(value):
    return lax.optimization_barrier(value.astype(jnp.bfloat16))

def device_partials(left, right):
    blocks = left.shape[0] // TOK_DEV
    lhs = left.reshape(blocks, TOK_DEV, -1).astype(jnp.float32)
    rhs = right.reshape(blocks, TOK_DEV, -1).astype(jnp.float32)
    terms = jnp.einsum('btf,btg->bfg', lhs, rhs)
    rounded = kept_bfloat16(terms)
    return lax.optimization_barrier(jnp.sum(rounded.astype(jnp.float32), axis=0))

def layer_sequence(block_row, segment_row, position_row, cot_row, weights):
    w_query, key_projection, value_projection, w_out, w_gate, w_up, w_down, attn_gain, mlp_gain, query_gain, key_norm_gain = weights
    sequence_length = block_row.shape[0]
    head_group = QUERY_HEADS // KEY_VALUE_HEADS
    factor = HEAD_SIZE ** (-0.5)
    resid = block_row.astype(jnp.float32)
    scale_one = inv_rms(resid)
    normed_rows = (resid * scale_one * attn_gain).astype(jnp.bfloat16)
    q_raw = jnp.dot(normed_rows, w_query, preferred_element_type=jnp.float32).reshape(sequence_length, QUERY_HEADS, HEAD_SIZE)
    key_unnormed = jnp.dot(normed_rows, key_projection, preferred_element_type=jnp.float32).reshape(sequence_length, KEY_VALUE_HEADS, HEAD_SIZE)
    value_rows = kept_bfloat16(jnp.dot(normed_rows, value_projection, preferred_element_type=jnp.float32)).reshape(sequence_length, KEY_VALUE_HEADS, HEAD_SIZE)
    values_wide = value_rows.astype(jnp.float32)
    q_scale = inv_rms(q_raw)
    key_scale = inv_rms(key_unnormed)
    q_normed = q_raw * q_scale * query_gain
    k_normed = key_unnormed * key_scale * key_norm_gain
    cos_tab, sin_tab = rope_tables(position_row, HEAD_SIZE)
    query_rotated = kept_bfloat16(q_normed * cos_tab + rotate(q_normed) * sin_tab)
    k_rot = kept_bfloat16(k_normed * cos_tab + rotate(k_normed) * sin_tab)
    query_group = query_rotated.astype(jnp.float32).reshape(sequence_length, KEY_VALUE_HEADS, head_group, HEAD_SIZE)
    k_wide = k_rot.astype(jnp.float32)
    index = jnp.arange(sequence_length, dtype=jnp.int32)
    allowed = (index[None, :] <= index[:, None]) & (segment_row[None, :] == segment_row[:, None])
    scores = jnp.einsum('nkgd,mkd->kgnm', query_group, k_wide) * factor
    scores = jnp.where(allowed[None, None], scores, NEG)
    top = lax.optimization_barrier(jnp.max(scores, axis=-1, keepdims=True))
    lse = top + jnp.log(lax.optimization_barrier(jnp.sum(jnp.exp(scores - top), axis=-1, keepdims=True)))
    probs = jnp.exp(scores - lse)
    probs_wide = kept_bfloat16(probs).astype(jnp.float32)
    attn_out = jnp.einsum('kgnm,mkd->nkgd', probs_wide, values_wide).astype(jnp.bfloat16).reshape(sequence_length, QUERY_HEADS * HEAD_SIZE)
    mid = resid + jnp.dot(attn_out, w_out, preferred_element_type=jnp.float32)
    scale_two = inv_rms(mid)
    normed_two = (mid * scale_two * mlp_gain).astype(jnp.bfloat16)
    gate = jnp.dot(normed_two, w_gate, preferred_element_type=jnp.float32)
    up = jnp.dot(normed_two, w_up, preferred_element_type=jnp.float32)
    sig = jax.nn.sigmoid(gate)
    hidden = (gate * sig * up).astype(jnp.bfloat16)
    block_out = (mid + jnp.dot(hidden, w_down, preferred_element_type=jnp.float32)).astype(jnp.bfloat16)
    d_hidden = jnp.dot(cot_row, w_down.T, preferred_element_type=jnp.float32)
    grad_down = device_partials(hidden, cot_row)
    d_gate = (d_hidden * up * sig * (1.0 + gate * (1.0 - sig))).astype(jnp.bfloat16)
    d_up = (d_hidden * gate * sig).astype(jnp.bfloat16)
    grad_gate = device_partials(normed_two, d_gate)
    grad_up = device_partials(normed_two, d_up)
    d_normed_two = jnp.dot(d_gate, w_gate.T, preferred_element_type=jnp.float32) + jnp.dot(d_up, w_up.T, preferred_element_type=jnp.float32)
    grad_mlp_gain = lax.optimization_barrier(jnp.sum(d_normed_two * mid * scale_two, axis=0))
    d_mid = cot_row.astype(jnp.float32) + norm_backward(d_normed_two, mid, scale_two, mlp_gain)
    d_mid_b = d_mid.astype(jnp.bfloat16)
    grad_out = device_partials(attn_out, d_mid_b)
    attention_gradient = kept_bfloat16(jnp.dot(d_mid_b, w_out.T, preferred_element_type=jnp.float32))
    grouped_gradient = attention_gradient.astype(jnp.float32).reshape(sequence_length, KEY_VALUE_HEADS, head_group, HEAD_SIZE)
    d_prob = jnp.einsum('nkgd,mkd->kgnm', grouped_gradient, values_wide)
    d_scores = kept_bfloat16(probs * (d_prob - lax.optimization_barrier(jnp.sum(probs * d_prob, axis=-1, keepdims=True))) * factor).astype(jnp.float32)
    d_qrot = jnp.einsum('kgnm,mkd->nkgd', d_scores, k_wide).reshape(sequence_length, QUERY_HEADS, HEAD_SIZE)
    d_krot = jnp.einsum('kgnm,nkgd->mkd', d_scores, query_group)
    values_gradient = jnp.einsum('kgnm,nkgd->mkd', probs_wide, grouped_gradient)
    d_qnormed = d_qrot * cos_tab + rotate_back(d_qrot * sin_tab)
    normed_key_gradient = d_krot * cos_tab + rotate_back(d_krot * sin_tab)
    grad_query_gain = lax.optimization_barrier(jnp.sum(d_qnormed * q_raw * q_scale, axis=(0, 1)))
    grad_key_gain = lax.optimization_barrier(jnp.sum(normed_key_gradient * key_unnormed * key_scale, axis=(0, 1)))
    d_query = norm_backward(d_qnormed, q_raw, q_scale, query_gain).astype(jnp.bfloat16).reshape(sequence_length, QUERY_HEADS * HEAD_SIZE)
    key_gradient = norm_backward(normed_key_gradient, key_unnormed, key_scale, key_norm_gain).astype(jnp.bfloat16).reshape(sequence_length, KEY_VALUE_HEADS * HEAD_SIZE)
    value_gradient = values_gradient.astype(jnp.bfloat16).reshape(sequence_length, KEY_VALUE_HEADS * HEAD_SIZE)
    grad_query = device_partials(normed_rows, d_query)
    grad_key = device_partials(normed_rows, key_gradient)
    grad_value = device_partials(normed_rows, value_gradient)
    d_normed = jnp.dot(d_query, w_query.T, preferred_element_type=jnp.float32)
    d_normed = d_normed + jnp.dot(key_gradient, key_projection.T, preferred_element_type=jnp.float32)
    d_normed = d_normed + jnp.dot(value_gradient, value_projection.T, preferred_element_type=jnp.float32)
    grad_attn_gain = lax.optimization_barrier(jnp.sum(d_normed * resid * scale_one, axis=0))
    d_block_in = d_mid + norm_backward(d_normed, resid, scale_one, attn_gain)
    grads = (grad_query, grad_key, grad_value, grad_out, grad_gate, grad_up, grad_down, grad_attn_gain, grad_mlp_gain, grad_query_gain, grad_key_gain)
    return (block_out, d_block_in, grads)

def reference(block_in, w_query, key_projection, value_projection, w_out, w_gate, w_up, w_down, attn_gain, mlp_gain, query_gain, key_norm_gain, segment_ids, positions, cotangent):
    weights = (w_query, key_projection, value_projection, w_out, w_gate, w_up, w_down, attn_gain, mlp_gain, query_gain, key_norm_gain)
    block_rows = block_in.reshape(NSEQ, LEN, MODEL_WIDTH)
    position_rows = positions.reshape(NSEQ, LEN)
    cot_rows = cotangent.reshape(NSEQ, LEN, MODEL_WIDTH)
    start = tuple((jnp.zeros(weight.shape, jnp.float32) for weight in weights))

    def advance(carry, item):
        block_row, segment_row, position_row, cot_row = item
        out_row, din_row, grads = layer_sequence(block_row, segment_row, position_row, cot_row, weights)
        return (tuple((total + grad for total, grad in zip(carry, grads))), (out_row, din_row))
    totals, (out_rows, din_rows) = lax.scan(advance, start, (block_rows, segment_ids, position_rows, cot_rows))
    return (out_rows.reshape(TOKENS, MODEL_WIDTH), din_rows.reshape(TOKENS, MODEL_WIDTH), totals[0], totals[1], totals[2], totals[3], totals[4], totals[5], totals[6], totals[7], totals[8], totals[9], totals[10])
```

```python
import functools

import jax
import jax.numpy as jnp
import numpy as np
from jax import lax
from jax.experimental import pallas as pl
from jax.experimental.pallas import tpu as pltpu
from jax.sharding import PartitionSpec as P

QUERY_HEADS = 16
KEY_VALUE_HEADS = 8
HEAD_SIZE = 128
GROUP = QUERY_HEADS // KEY_VALUE_HEADS

EPS = 1e-06
THETA = 1000000.0
NEG = -1e30


F32 = jnp.float32
BF16 = jnp.bfloat16


def inv_rms(value):
    return lax.rsqrt(jnp.mean(value * value, axis=-1, keepdims=True) + EPS)


def norm_backward(grad, value, scale, gain):
    upstream = grad * gain
    return scale * (
        upstream - value * scale * scale * jnp.mean(upstream * value, axis=-1, keepdims=True)
    )


def dot_nn(left, right):
    return lax.dot_general(left, right, (((1,), (0,)), ((), ())), preferred_element_type=F32)


def dot_nt(left, right):
    return lax.dot_general(left, right, (((1,), (1,)), ((), ())), preferred_element_type=F32)


def dot_tn(left, right, dtype=F32):
    return lax.dot_general(left, right, (((0,), (0,)), ((), ())), preferred_element_type=dtype)


def rope_tables(position_row, width):
    half = width // 2
    freq = jnp.exp(
        -(jnp.arange(half, dtype=F32) * (2.0 / width)) * jnp.log(jnp.float32(THETA))
    )
    angle = position_row.astype(F32)[:, None] * freq[None, :]
    cos, sin = jnp.cos(angle), jnp.sin(angle)
    return jnp.concatenate([cos, cos], axis=-1), jnp.concatenate([-sin, sin], axis=-1)


def _half_turn(value):
    return pltpu.roll(value, HEAD_SIZE // 2, axis=1)


def _rotated(raw, gain, cos, sin):
    scale = inv_rms(raw)
    normed = raw * scale * gain
    return (normed * cos + _half_turn(normed) * sin).astype(BF16), scale


def _scores(q_rot, k_rot, mask):
    scores = dot_nt(q_rot, k_rot) * HEAD_SIZE ** (-0.5)
    scores = jnp.where(mask > 0.5, scores, NEG)
    top = jnp.max(scores, axis=-1, keepdims=True)
    lse = top + jnp.log(jnp.sum(jnp.exp(scores - top), axis=-1, keepdims=True))
    return jnp.exp(scores - lse)


def _head(block, index):
    return block[:, index * HEAD_SIZE : (index + 1) * HEAD_SIZE]


def attention_kernel(qkv, cos, sin, mask, q_gain, k_gain, out):
    block = qkv[...]
    k_rot, _ = _rotated(_head(block, GROUP), k_gain[...], cos[...], sin[...])
    values = _head(block, GROUP + 1).astype(BF16)
    for h in range(GROUP):
        q_rot, _ = _rotated(_head(block, h), q_gain[...], cos[...], sin[...])
        probs = _scores(q_rot, k_rot, mask[...]).astype(BF16)
        out[:, h * HEAD_SIZE : (h + 1) * HEAD_SIZE] = dot_nn(probs, values).astype(BF16)


def attention_back_kernel(
    qkv, cos_ref, sin_ref, mask_ref, q_gain, k_gain, d_attn, d_qkv, d_q_gain, d_k_gain
):
    block = qkv[...]
    cos, sin, mask = cos_ref[...], sin_ref[...], mask_ref[...]
    k_raw = _head(block, GROUP)
    k_rot, k_scale = _rotated(k_raw, k_gain[...], cos, sin)
    values = _head(block, GROUP + 1).astype(BF16)
    d_k = jnp.zeros(k_raw.shape, F32)
    d_v = jnp.zeros(k_raw.shape, F32)
    gain_sum = jnp.zeros((1, HEAD_SIZE), F32)
    for h in range(GROUP):
        q_raw = _head(block, h)
        q_rot, q_scale = _rotated(q_raw, q_gain[...], cos, sin)
        probs = _scores(q_rot, k_rot, mask)
        grad = d_attn[:, h * HEAD_SIZE : (h + 1) * HEAD_SIZE]
        d_prob = dot_nt(grad, values)
        d_scores = (
            probs
            * (d_prob - jnp.sum(probs * d_prob, axis=-1, keepdims=True))
            * HEAD_SIZE ** (-0.5)
        ).astype(BF16)
        d_q = dot_nn(d_scores, k_rot)
        d_k += dot_tn(d_scores, q_rot)
        d_v += dot_tn(probs.astype(BF16), grad)
        d_normed = d_q * cos - _half_turn(d_q) * sin
        gain_sum += jnp.sum(d_normed * q_raw * q_scale, axis=0, keepdims=True)
        d_qkv[:, h * HEAD_SIZE : (h + 1) * HEAD_SIZE] = norm_backward(
            d_normed, q_raw, q_scale, q_gain[...]
        ).astype(BF16)
    d_normed = d_k * cos - _half_turn(d_k) * sin
    d_q_gain[0] = gain_sum
    d_k_gain[0] = jnp.sum(d_normed * k_raw * k_scale, axis=0, keepdims=True)
    d_qkv[:, GROUP * HEAD_SIZE : (GROUP + 1) * HEAD_SIZE] = norm_backward(
        d_normed, k_raw, k_scale, k_gain[...]
    ).astype(BF16)
    d_qkv[:, (GROUP + 1) * HEAD_SIZE :] = d_v.astype(BF16)


def _whole(shape):
    return pl.BlockSpec(shape, lambda g: (0,) * len(shape))


def attention(qkv, cos, sin, mask, q_gain, k_gain):
    tokens, width = qkv.shape
    packed = (GROUP + 2) * HEAD_SIZE
    groups = width // packed
    return pl.pallas_call(
        attention_kernel,
        grid=(groups,),
        in_specs=[
            pl.BlockSpec((tokens, packed), lambda g: (0, g)),
            _whole(cos.shape),
            _whole(sin.shape),
            _whole(mask.shape),
            _whole(q_gain.shape),
            _whole(k_gain.shape),
        ],
        out_specs=pl.BlockSpec((tokens, GROUP * HEAD_SIZE), lambda g: (0, g)),
        out_shape=jax.ShapeDtypeStruct((tokens, groups * GROUP * HEAD_SIZE), BF16),
        name="attention",
    )(qkv, cos, sin, mask, q_gain, k_gain)


def attention_back(qkv, cos, sin, mask, q_gain, k_gain, d_attn):
    tokens, width = qkv.shape
    packed = (GROUP + 2) * HEAD_SIZE
    groups = width // packed
    return pl.pallas_call(
        attention_back_kernel,
        grid=(groups,),
        in_specs=[
            pl.BlockSpec((tokens, packed), lambda g: (0, g)),
            _whole(cos.shape),
            _whole(sin.shape),
            _whole(mask.shape),
            _whole(q_gain.shape),
            _whole(k_gain.shape),
            pl.BlockSpec((tokens, GROUP * HEAD_SIZE), lambda g: (0, g)),
        ],
        out_specs=[
            pl.BlockSpec((tokens, packed), lambda g: (0, g)),
            pl.BlockSpec((1, 1, HEAD_SIZE), lambda g: (g, 0, 0)),
            pl.BlockSpec((1, 1, HEAD_SIZE), lambda g: (g, 0, 0)),
        ],
        out_shape=[
            jax.ShapeDtypeStruct((tokens, width), BF16),
            jax.ShapeDtypeStruct((groups, 1, HEAD_SIZE), F32),
            jax.ShapeDtypeStruct((groups, 1, HEAD_SIZE), F32),
        ],
        name="attention_back",
    )(qkv, cos, sin, mask, q_gain, k_gain, d_attn)


def mlp_kernel(normed, cotangent, w_gu, w_down, hidden, d_gu, d_normed, down):
    unit = w_down.shape[0]

    @pl.when(pl.program_id(0) == 0)
    def _():
        d_normed[...] = jnp.zeros(d_normed.shape, F32)
        down[...] = jnp.zeros(down.shape, F32)

    gate_up = dot_nn(normed[...], w_gu[...])
    gate, up = gate_up[:, :unit], gate_up[:, unit:]
    d_hidden = dot_nt(cotangent[...], w_down[...])
    sig = jax.nn.sigmoid(gate)
    hid = (gate * sig * up).astype(BF16)
    hidden[...] = hid
    d_gu[:, :unit] = (d_hidden * up * sig * (1.0 + gate * (1.0 - sig))).astype(BF16)
    d_gu[:, unit:] = (d_hidden * gate * sig).astype(BF16)
    d_normed[...] += dot_nt(d_gu[...], w_gu[...])
    down[...] += dot_nn(hid, w_down[...])


def mlp(normed, cotangent, w_gu, w_down, unit):
    tokens, width = normed.shape
    ff = w_down.shape[0]
    return pl.pallas_call(
        mlp_kernel,
        grid=(ff // unit,),
        in_specs=[
            _whole(normed.shape),
            _whole(cotangent.shape),
            pl.BlockSpec((width, 2 * unit), lambda g: (0, g)),
            pl.BlockSpec((unit, width), lambda g: (g, 0)),
        ],
        out_specs=[
            pl.BlockSpec((tokens, unit), lambda g: (0, g)),
            pl.BlockSpec((tokens, 2 * unit), lambda g: (0, g)),
            _whole((tokens, width)),
            _whole((tokens, width)),
        ],
        out_shape=[
            jax.ShapeDtypeStruct((tokens, ff), BF16),
            jax.ShapeDtypeStruct((tokens, 2 * ff), BF16),
            jax.ShapeDtypeStruct((tokens, width), F32),
            jax.ShapeDtypeStruct((tokens, width), F32),
        ],
        name="mlp",
    )(normed, cotangent, w_gu, w_down)


def unpack_kernel(parts, place_ref, own, sibling, *outs):
    mine = pl.program_id(0) == 0

    def write(block):
        start = 0
        for out, width in zip(outs, parts):
            out[...] = block[:, start : start + width].astype(F32)
            start += width

    @pl.when(mine)
    def _():
        write(own[0])

    @pl.when(jnp.logical_not(mine))
    def _():
        write(sibling[0])


def unpack(own, sibling, place, parts, cores):
    blocks, rows, width = own.shape
    unit = sum(parts)
    if width % unit:
        full = jnp.zeros((rows, cores * blocks * width), BF16)
        for i, piece in enumerate([*own, *sibling][: cores * blocks]):
            full = lax.dynamic_update_slice(full, piece, (0, place[i] * width))
        outs, start = [], 0
        for part in parts:
            outs.append(
                jnp.concatenate(
                    [full[:, i + start : i + start + part] for i in range(0, full.shape[1], unit)],
                    axis=1,
                ).astype(F32)
            )
            start += part
        return outs
    units = width // unit

    def source(which):
        def index(c, b, u, place_ref):
            here = c == which
            fixed_b, fixed_u = (blocks - 1, units - 1) if which == 0 else (0, 0)
            return jnp.where(here, b, fixed_b), 0, jnp.where(here, u, fixed_u)

        return index

    def target(c, b, u, place_ref):
        return 0, place_ref[c * blocks + b] * units + u

    return pl.pallas_call(
        functools.partial(unpack_kernel, parts),
        grid_spec=pltpu.PrefetchScalarGridSpec(
            num_scalar_prefetch=1,
            grid=(cores, blocks, units),
            in_specs=[
                pl.BlockSpec((1, rows, unit), source(0)),
                pl.BlockSpec((1, rows, unit), source(1)),
            ],
            out_specs=[pl.BlockSpec((rows, part), target) for part in parts],
        ),
        out_shape=[
            jax.ShapeDtypeStruct((rows, cores * blocks * units * part), F32) for part in parts
        ],
        name="unpack",
    )(place, own, sibling)


def chip_cycle(mesh):
    column = mesh.devices.reshape(mesh.shape["replica"], mesh.shape["fsdp"])[:, 0]
    total = len(column)
    coords = [tuple(getattr(d, "coords", None) or ()) for d in column]
    cores = 1
    if all(coords):
        while cores < total and coords[cores] == coords[0]:
            cores += 1
    chips = coords[::cores]
    count = len(chips)
    order = list(range(count))
    if count * cores == total and len(set(chips)) == count and all(chips):
        varying = [a for a in range(3) if len({c[a] for c in chips}) > 1]
        if len(varying) == 2:
            values = [sorted({c[a] for c in chips}) for a in varying]
            place = {
                tuple(values[i].index(c[a]) for i, a in enumerate(varying)): k
                for k, c in enumerate(chips)
            }
            high, wide = len(values[0]), len(values[1])
            if high * wide == count:
                if high % 2:
                    place = {(b, a): k for (a, b), k in place.items()}
                    high, wide = wide, high
                if high % 2 == 0:
                    walk = []
                    for row in range(high):
                        cols = range(1, wide) if row % 2 == 0 else range(wide - 1, 0, -1)
                        walk += [(row, col) for col in cols]
                    walk += [(row, 0) for row in range(high - 1, -1, -1)]
                    order = [place[w] for w in walk]
    return cores, order


class Links:
    def __init__(self, mesh):
        self.ranks = mesh.shape["fsdp"]
        self.replicas = mesh.shape["replica"]
        self.cores, self.cycle = chip_cycle(mesh)
        self.chips = len(self.cycle)
        table = np.zeros((self.chips,), np.int32)
        for place, chip in enumerate(self.cycle):
            table[chip] = place
        self.table = table

    def start(self):
        self.rank = lax.axis_index("fsdp")
        replica = lax.axis_index("replica")
        self.core = replica % self.cores
        self.place = jnp.asarray(self.table)[replica // self.cores]

    def from_rank(self, value, shift):
        pairs = [(i, (i - shift) % self.ranks) for i in range(self.ranks)]
        return lax.ppermute(value, "fsdp", pairs)

    def others(self, value):
        return [self.from_rank(value, s) for s in range(1, self.ranks)]

    def sibling(self, value):
        pairs = [
            (chip * self.cores + core, chip * self.cores + (core + 1) % self.cores)
            for chip in range(self.chips)
            for core in range(self.cores)
        ]
        return lax.ppermute(value, "replica", pairs)

    def along(self, value, direction):
        pairs = [
            (
                self.cycle[i] * self.cores + core,
                self.cycle[(i + direction) % self.chips] * self.cores + core,
            )
            for i in range(self.chips)
            for core in range(self.cores)
        ]
        return lax.ppermute(value, "replica", pairs)

    def total(self, value):
        for axis, size in (("replica", self.replicas), ("fsdp", self.ranks)):
            if size & (size - 1):
                value = lax.psum(value, axis)
                continue
            step = 1
            while step < size:
                value = value + lax.ppermute(value, axis, [(i, i ^ step) for i in range(size)])
                step *= 2
        return value

    def reduce(self, grad, exchange):
        blocks, rows, width = grad.shape
        chips = self.chips
        seg = rows // (2 * chips)
        result = jnp.zeros(grad.shape, BF16)
        for turn, direction in enumerate((1, -1)):
            q = self.place if direction == 1 else (chips - self.place) % chips
            base = turn * chips

            def row(index):
                return (base + lax.rem(index + 2 * chips, chips)) * seg

            def local(index):
                return lax.dynamic_slice(grad, (0, row(index), 0), (blocks, seg, width))

            held = local(q)
            for step in range(chips - 1):
                held = self.along(held, direction)
                held = (held.astype(F32) + local(q - step - 1).astype(F32)).astype(BF16)
            if exchange:
                held = self.swap(held)
            result = lax.dynamic_update_slice(result, held, (0, row(q + 1), 0))
            for step in range(chips - 1):
                held = self.along(held, direction)
                result = lax.dynamic_update_slice(result, held, (0, row(q - step), 0))
        return result

    def swap(self, value):
        pieces = [lax.dynamic_slice_in_dim(value, self.rank, 1, 0)]
        for s in range(1, self.ranks):
            to = (self.rank - s + self.ranks) % self.ranks
            pieces.append(self.from_rank(lax.dynamic_slice_in_dim(value, to, 1, 0), s))
        return jnp.concatenate(pieces, axis=0)


def packed_columns(arrays, units, index, count):
    blocks = [
        lax.dynamic_slice_in_dim(a, index * (a.shape[1] // count), a.shape[1] // count, 1)
        for a in arrays
    ]
    steps = blocks[0].shape[1] // units[0]
    return jnp.concatenate(
        [b[:, i * u : (i + 1) * u] for i in range(steps) for b, u in zip(blocks, units)], axis=1
    )


def shards(
    links,
    block_in,
    w_query,
    key_projection,
    value_projection,
    w_out,
    w_gate,
    w_up,
    w_down,
    attn_gain,
    mlp_gain,
    query_gain,
    key_norm_gain,
    segment_ids,
    positions,
    cotangent,
):
    links.start()
    ranks, cores = links.ranks, links.cores
    rank, core = links.rank, links.core
    tokens, width = block_in.shape
    sequence = tokens * ranks
    segment_row = segment_ids[0]

    hidden_units = w_down.shape[0]
    unit = 256 if hidden_units % 512 == 0 else 128
    qkv_units = (GROUP * HEAD_SIZE, HEAD_SIZE, HEAD_SIZE)

    def column_block(arrays, units, after):
        rows = arrays[0].shape[0]
        half = rows // cores
        own = packed_columns(arrays, units, rank, ranks)
        full = jnp.zeros((rows * ranks, own.shape[1]), BF16)
        full = lax.dynamic_update_slice(full, own, (rank * rows, 0))
        for s in range(1, ranks):
            to = (rank - s + ranks) % ranks
            part = [lax.dynamic_slice_in_dim(a, core * half, half, 0) for a in arrays]
            sent = packed_columns(part, units, to, ranks)
            if after is not None:
                sent, _ = lax.optimization_barrier((sent, after))
            piece = links.from_rank(sent, s)
            base = ((rank + s) % ranks) * rows
            held = core
            for turn in range(cores):
                full = lax.dynamic_update_slice(full, piece, (base + held * half, 0))
                if turn + 1 < cores:
                    piece = links.sibling(piece)
                    held = (held - 1 + cores) % cores
        return full

    rows_in = jnp.concatenate([block_in] + links.others(block_in), axis=0)
    position_row = jnp.concatenate([positions] + links.others(positions), axis=0)
    w_qkv = column_block((w_query, key_projection, value_projection), qkv_units, None)
    cot = jnp.concatenate([cotangent] + links.others(cotangent), axis=0)
    w_gu = column_block((w_gate, w_up), (unit, unit), rows_in[:8, :128])

    offset = rank * tokens
    token = lax.rem(offset + jnp.arange(sequence, dtype=jnp.int32), sequence)
    segments = lax.dynamic_slice_in_dim(
        jnp.concatenate([segment_row, segment_row]), offset, sequence
    )
    mask = (
        (token[None, :] <= token[:, None]) & (segments[None, :] == segments[:, None])
    ).astype(F32)
    cos_tab, sin_tab = rope_tables(position_row, HEAD_SIZE)
    q_gain, k_gain = query_gain[None, :], key_norm_gain[None, :]

    resid = rows_in.astype(F32)
    scale_one = inv_rms(resid)
    normed = (resid * scale_one * attn_gain).astype(BF16)
    qkv = dot_nn(normed, w_qkv)
    attn_out = attention(qkv, cos_tab, sin_tab, mask, q_gain, k_gain)
    mid_part = dot_nn(attn_out, w_out)

    def all_summed(part):
        total = part
        sent = part.astype(BF16)
        for s in range(1, ranks):
            got = links.from_rank(sent, s)
            total = total + jnp.roll(got, s * tokens, axis=0).astype(F32)
        return total

    def own_summed(part):
        total = part[:tokens]
        for s in range(1, ranks):
            far = (ranks - s) * tokens
            total = total + links.from_rank(part[far : far + tokens].astype(BF16), s).astype(F32)
        return total

    mid = resid + all_summed(mid_part)
    scale_two = inv_rms(mid)
    normed_two = (mid * scale_two * mlp_gain).astype(BF16)
    hidden, d_gu, d_normed_part, down_part = mlp(normed_two, cot, w_gu, w_down, unit)

    d_normed_two = all_summed(d_normed_part)

    def both(value):
        return jnp.concatenate([value, links.sibling(value)], axis=0) if cores > 1 else value

    def both_of_columns(value):
        size = value.shape[1] // cores
        own = lax.dynamic_slice_in_dim(value, core * size, size, 1)
        if cores == 1:
            return own
        theirs = lax.dynamic_slice_in_dim(value, ((core + 1) % cores) * size, size, 1)
        return jnp.concatenate([own, links.sibling(theirs)], axis=0)

    grad_gu = dot_tn(both(normed_two), both_of_columns(d_gu), BF16)
    grad_down = dot_tn(both_of_columns(hidden), both(cot), BF16)
    sum_gu = links.reduce(grad_gu.reshape(ranks, width // ranks, -1), True)
    sum_down = links.reduce(grad_down[None], False)

    grad_mlp_gain = jnp.sum((d_normed_two * mid * scale_two)[:tokens], axis=0)
    d_mid = cot.astype(F32) + norm_backward(d_normed_two, mid, scale_two, mlp_gain)
    d_mid_b = d_mid.astype(BF16)
    d_attn = dot_nt(d_mid_b, w_out).astype(BF16)
    d_qkv, d_q_gain, d_k_gain = attention_back(
        qkv, cos_tab, sin_tab, mask, q_gain, k_gain, d_attn
    )
    grad_out = dot_tn(both_of_columns(attn_out), both(d_mid_b), BF16)
    grad_qkv = dot_tn(both(normed), both_of_columns(d_qkv), BF16)
    sum_qkv = links.reduce(grad_qkv.reshape(ranks, width // ranks, -1), True)
    sum_out = links.reduce(grad_out[None], False)

    d_normed = own_summed(dot_nt(d_qkv, w_qkv))
    resid_own, scale_own = resid[:tokens], scale_one[:tokens]
    grad_attn_gain = jnp.sum(d_normed * resid_own * scale_own, axis=0)
    d_block_in = d_mid[:tokens] + norm_backward(d_normed, resid_own, scale_own, attn_gain)
    block_out = (mid[:tokens] + own_summed(down_part)).astype(BF16)

    gains = links.total(
        jnp.concatenate(
            [
                grad_attn_gain,
                grad_mlp_gain,
                jnp.sum(d_q_gain, axis=(0, 1)),
                jnp.sum(d_k_gain, axis=(0, 1)),
            ]
        ).reshape(-1, HEAD_SIZE)
    ).reshape(-1)

    turns = (core + jnp.arange(cores, dtype=jnp.int32)) % cores
    origin = (rank + jnp.arange(ranks, dtype=jnp.int32)) % ranks
    place = (origin[None, :] * cores + turns[:, None]).reshape(-1)

    def columns(summed, parts):
        other = links.sibling(summed) if cores > 1 else summed
        return unpack(summed, other, place, parts, cores)

    def stacked(summed):
        summed = summed[0]
        if cores == 1:
            return summed.astype(F32)
        other = links.sibling(summed)
        return jnp.where(
            core == 0,
            jnp.concatenate([summed, other], axis=0),
            jnp.concatenate([other, summed], axis=0),
        ).astype(F32)

    total_gate, total_up = columns(sum_gu, (unit, unit))
    total_query, total_key, total_value = columns(sum_qkv, qkv_units)
    return (
        block_out,
        d_block_in,
        total_query,
        total_key,
        total_value,
        stacked(sum_out),
        total_gate,
        total_up,
        stacked(sum_down),
        gains[:width],
        gains[width : 2 * width],
        gains[2 * width : 2 * width + HEAD_SIZE],
        gains[2 * width + HEAD_SIZE :],
    )


def solution(mesh):
    rows = P(("replica", "fsdp"), None)
    weight = P("fsdp", None)
    in_specs = (
        (rows,)
        + (weight,) * 7
        + (P(),) * 4
        + (P("replica", None), P(("replica", "fsdp")), rows)
    )
    out_specs = (rows, rows) + (weight,) * 7 + (P(),) * 4
    return jax.shard_map(
        functools.partial(shards, Links(mesh)),
        mesh=mesh,
        in_specs=in_specs,
        out_specs=out_specs,
        check_vma=False,
    )
```

```python
import functools

import jax
import jax.numpy as jnp
import numpy as np
from jax import lax
from jax.experimental import pallas as pl
from jax.experimental.pallas import tpu as pltpu
from jax.sharding import PartitionSpec as P

QUERY_HEADS = 16
KEY_VALUE_HEADS = 8
HEAD_SIZE = 128
GROUP = QUERY_HEADS // KEY_VALUE_HEADS

EPS = 1e-06
THETA = 1000000.0
NEG = -1e30


F32 = jnp.float32
BF16 = jnp.bfloat16


def inv_rms(value):
    return lax.rsqrt(jnp.mean(value * value, axis=-1, keepdims=True) + EPS)


def norm_backward(grad, value, scale, gain):
    upstream = grad * gain
    return scale * (
        upstream - value * scale * scale * jnp.mean(upstream * value, axis=-1, keepdims=True)
    )


def dot_nn(left, right):
    return lax.dot_general(left, right, (((1,), (0,)), ((), ())), preferred_element_type=F32)


def dot_nt(left, right):
    return lax.dot_general(left, right, (((1,), (1,)), ((), ())), preferred_element_type=F32)


def dot_tn(left, right, dtype=F32):
    return lax.dot_general(left, right, (((0,), (0,)), ((), ())), preferred_element_type=dtype)


def rope_tables(position_row, width):
    half = width // 2
    freq = jnp.exp(
        -(jnp.arange(half, dtype=F32) * (2.0 / width)) * jnp.log(jnp.float32(THETA))
    )
    angle = position_row.astype(F32)[:, None] * freq[None, :]
    cos, sin = jnp.cos(angle), jnp.sin(angle)
    return jnp.concatenate([cos, cos], axis=-1), jnp.concatenate([-sin, sin], axis=-1)


def _half_turn(value):
    return pltpu.roll(value, HEAD_SIZE // 2, axis=1)


def _rotated(raw, gain, cos, sin):
    scale = inv_rms(raw)
    normed = raw * scale * gain
    return (normed * cos + _half_turn(normed) * sin).astype(BF16), scale


def _probs(q_rot, k_rot, mask):
    scores = dot_nt(q_rot, k_rot) * HEAD_SIZE ** (-0.5)
    scores = jnp.where(mask > 0.5, scores, NEG)
    top = jnp.max(scores, axis=-1, keepdims=True)
    lse = top + jnp.log(jnp.sum(jnp.exp(scores - top), axis=-1, keepdims=True))
    return jnp.exp(scores - lse)


def _head(index):
    return pl.ds(index * HEAD_SIZE, HEAD_SIZE)


def _row_chunks(rows, body):
    chunk = min(rows, 256)
    if rows == chunk:
        body(pl.ds(0, rows))
    else:

        def step(i, carry):
            body(pl.ds(pl.multiple_of(i * chunk, chunk), chunk))
            return carry

        lax.fori_loop(0, rows // chunk, step, 0)


def attention_kernel(normed, w_qkv, cos, sin, mask, q_gain, k_gain, out, qkv, k_scr, v_scr):
    def project(rows):
        block = dot_nn(normed[rows, :], w_qkv[...])
        qkv[rows, :] = block
        k_raw = block[:, GROUP * HEAD_SIZE : (GROUP + 1) * HEAD_SIZE]
        k_scr[rows, :], _ = _rotated(k_raw, k_gain[...], cos[rows, :], sin[rows, :])
        v_scr[rows, :] = block[:, (GROUP + 1) * HEAD_SIZE :].astype(BF16)

    def attend(rows):
        for h in range(GROUP):
            q_rot, _ = _rotated(qkv[rows, _head(h)], q_gain[...], cos[rows, :], sin[rows, :])
            probs = _probs(q_rot, k_scr[...], mask[rows, :]).astype(BF16)
            out[rows, _head(h)] = dot_nn(probs, v_scr[...]).astype(BF16)

    _row_chunks(normed.shape[0], project)
    _row_chunks(normed.shape[0], attend)


def attention_back_kernel(
    qkv, cos, sin, mask, q_gain, k_gain, d_attn, d_qkv, d_q_gain, d_k_gain, k_scr, v_scr, dk_scr, dv_scr
):
    total = qkv.shape[0]

    def prepare(rows):
        k_scr[rows, :], _ = _rotated(qkv[rows, _head(GROUP)], k_gain[...], cos[rows, :], sin[rows, :])
        v_scr[rows, :] = qkv[rows, _head(GROUP + 1)].astype(BF16)
        dk_scr[rows, :] = jnp.zeros((rows.size, HEAD_SIZE), F32)
        dv_scr[rows, :] = jnp.zeros((rows.size, HEAD_SIZE), F32)

    def queries(rows):
        for h in range(GROUP):
            q_raw = qkv[rows, _head(h)]
            q_rot, q_scale = _rotated(q_raw, q_gain[...], cos[rows, :], sin[rows, :])
            probs = _probs(q_rot, k_scr[...], mask[rows, :])
            grad = d_attn[rows, _head(h)]
            d_prob = dot_nt(grad, v_scr[...])
            d_scores = (
                probs
                * (d_prob - jnp.sum(probs * d_prob, axis=-1, keepdims=True))
                * HEAD_SIZE ** (-0.5)
            ).astype(BF16)
            d_q = dot_nn(d_scores, k_scr[...])
            dk_scr[...] += dot_tn(d_scores, q_rot)
            dv_scr[...] += dot_tn(probs.astype(BF16), grad)
            d_normed = d_q * cos[rows, :] - _half_turn(d_q) * sin[rows, :]
            d_q_gain[0] += jnp.sum(d_normed * q_raw * q_scale, axis=0, keepdims=True)
            d_qkv[rows, _head(h)] = norm_backward(d_normed, q_raw, q_scale, q_gain[...]).astype(BF16)

    def keys(rows):
        k_raw = qkv[rows, _head(GROUP)]
        k_scale = inv_rms(k_raw)
        d_k = dk_scr[rows, :]
        d_normed = d_k * cos[rows, :] - _half_turn(d_k) * sin[rows, :]
        d_k_gain[0] += jnp.sum(d_normed * k_raw * k_scale, axis=0, keepdims=True)
        d_qkv[rows, _head(GROUP)] = norm_backward(d_normed, k_raw, k_scale, k_gain[...]).astype(BF16)
        d_qkv[rows, _head(GROUP + 1)] = dv_scr[rows, :].astype(BF16)

    d_q_gain[...] = jnp.zeros(d_q_gain.shape, F32)
    d_k_gain[...] = jnp.zeros(d_k_gain.shape, F32)
    _row_chunks(total, prepare)
    _row_chunks(total, queries)
    _row_chunks(total, keys)


def _whole(shape):
    return pl.BlockSpec(shape, lambda *g: (0,) * len(shape))


def attention(normed, w_qkv, cos, sin, mask, q_gain, k_gain):
    tokens, wide = normed.shape
    width = w_qkv.shape[1]
    packed = (GROUP + 2) * HEAD_SIZE
    groups = width // packed
    return pl.pallas_call(
        attention_kernel,
        grid=(groups,),
        in_specs=[
            _whole(normed.shape),
            pl.BlockSpec((wide, packed), lambda g: (0, g)),
            _whole(cos.shape),
            _whole(sin.shape),
            _whole(mask.shape),
            _whole(q_gain.shape),
            _whole(k_gain.shape),
        ],
        out_specs=[
            pl.BlockSpec((tokens, GROUP * HEAD_SIZE), lambda g: (0, g)),
            pl.BlockSpec((tokens, packed), lambda g: (0, g)),
        ],
        out_shape=[
            jax.ShapeDtypeStruct((tokens, groups * GROUP * HEAD_SIZE), BF16),
            jax.ShapeDtypeStruct((tokens, width), F32),
        ],
        scratch_shapes=[pltpu.VMEM((tokens, HEAD_SIZE), BF16)] * 2,
        name="attention",
    )(normed, w_qkv, cos, sin, mask, q_gain, k_gain)


def attention_back(qkv, cos, sin, mask, q_gain, k_gain, d_attn):
    tokens, width = qkv.shape
    packed = (GROUP + 2) * HEAD_SIZE
    groups = width // packed
    return pl.pallas_call(
        attention_back_kernel,
        grid=(groups,),
        in_specs=[
            pl.BlockSpec((tokens, packed), lambda g: (0, g)),
            _whole(cos.shape),
            _whole(sin.shape),
            _whole(mask.shape),
            _whole(q_gain.shape),
            _whole(k_gain.shape),
            pl.BlockSpec((tokens, GROUP * HEAD_SIZE), lambda g: (0, g)),
        ],
        out_specs=[
            pl.BlockSpec((tokens, packed), lambda g: (0, g)),
            pl.BlockSpec((1, 1, HEAD_SIZE), lambda g: (g, 0, 0)),
            pl.BlockSpec((1, 1, HEAD_SIZE), lambda g: (g, 0, 0)),
        ],
        out_shape=[
            jax.ShapeDtypeStruct((tokens, width), BF16),
            jax.ShapeDtypeStruct((groups, 1, HEAD_SIZE), F32),
            jax.ShapeDtypeStruct((groups, 1, HEAD_SIZE), F32),
        ],
        scratch_shapes=[pltpu.VMEM((tokens, HEAD_SIZE), BF16)] * 2
        + [pltpu.VMEM((tokens, HEAD_SIZE), F32)] * 2,
        name="attention_back",
    )(qkv, cos, sin, mask, q_gain, k_gain, d_attn)


def mlp_kernel(normed, cotangent, w_gu, w_down, hidden, d_gu, d_normed, down):
    unit = w_down.shape[0]

    @pl.when(pl.program_id(0) == 0)
    def _():
        d_normed[...] = jnp.zeros(d_normed.shape, F32)
        down[...] = jnp.zeros(down.shape, F32)

    gate_up = dot_nn(normed[...], w_gu[...])
    gate, up = gate_up[:, :unit], gate_up[:, unit:]
    d_hidden = dot_nt(cotangent[...], w_down[...])
    sig = jax.nn.sigmoid(gate)
    hid = (gate * sig * up).astype(BF16)
    hidden[...] = hid
    d_gu[:, :unit] = (d_hidden * up * sig * (1.0 + gate * (1.0 - sig))).astype(BF16)
    d_gu[:, unit:] = (d_hidden * gate * sig).astype(BF16)
    d_normed[...] += dot_nt(d_gu[...], w_gu[...])
    down[...] += dot_nn(hid, w_down[...])


def mlp(normed, cotangent, w_gu, w_down, unit):
    tokens, width = normed.shape
    ff = w_down.shape[0]
    return pl.pallas_call(
        mlp_kernel,
        grid=(ff // unit,),
        in_specs=[
            _whole(normed.shape),
            _whole(cotangent.shape),
            pl.BlockSpec((width, 2 * unit), lambda g: (0, g)),
            pl.BlockSpec((unit, width), lambda g: (g, 0)),
        ],
        out_specs=[
            pl.BlockSpec((tokens, unit), lambda g: (0, g)),
            pl.BlockSpec((tokens, 2 * unit), lambda g: (0, g)),
            _whole((tokens, width)),
            _whole((tokens, width)),
        ],
        out_shape=[
            jax.ShapeDtypeStruct((tokens, ff), BF16),
            jax.ShapeDtypeStruct((tokens, 2 * ff), BF16),
            jax.ShapeDtypeStruct((tokens, width), F32),
            jax.ShapeDtypeStruct((tokens, width), F32),
        ],
        name="mlp",
    )(normed, cotangent, w_gu, w_down)


def pack_kernel(place_ref, *refs):
    arrays, out = refs[:-1], refs[-1]
    start = 0
    for a in arrays:
        out[:, start : start + a.shape[1]] = a[...]
        start += a.shape[1]


def pack(arrays, units, column, count, rows, from_row, to_row, out_rows):
    steps = arrays[0].shape[1] // count // units[0]
    place = jnp.stack([column * steps, from_row, to_row]).astype(jnp.int32)
    unit = sum(units)
    return pl.pallas_call(
        pack_kernel,
        grid_spec=pltpu.PrefetchScalarGridSpec(
            num_scalar_prefetch=1,
            grid=(steps,),
            in_specs=[
                pl.BlockSpec((rows, u), lambda i, place: (place[1], place[0] + i)) for u in units
            ],
            out_specs=pl.BlockSpec((rows, unit), lambda i, place: (place[2], i)),
        ),
        out_shape=jax.ShapeDtypeStruct((out_rows, steps * unit), BF16),
        name="pack",
    )(place, *arrays)


def insert_kernel(place_ref, *refs):
    count = len(refs) - 3
    pieces, full, sems = refs[:count], refs[-2], refs[-1]
    copies = []
    for i, piece in enumerate(pieces):
        rows = piece.shape[0]
        row = pl.multiple_of(place_ref[i] * rows, rows)
        copies.append(pltpu.make_async_copy(piece, full.at[pl.ds(row, rows), :], sems.at[i]))
    for c in copies:
        c.start()
    for c in copies:
        c.wait()


def insert(full, pieces, places):
    anywhere = pl.BlockSpec(memory_space=pl.ANY)
    return pl.pallas_call(
        insert_kernel,
        grid_spec=pltpu.PrefetchScalarGridSpec(
            num_scalar_prefetch=1,
            grid=(),
            in_specs=[anywhere] * (len(pieces) + 1),
            out_specs=anywhere,
            scratch_shapes=[pltpu.SemaphoreType.DMA((len(pieces),))],
        ),
        out_shape=jax.ShapeDtypeStruct(full.shape, full.dtype),
        input_output_aliases={len(pieces) + 1: 0},
        name="insert",
    )(jnp.stack(places).astype(jnp.int32), *pieces, full)


def unpack_kernel(parts, turned, place_ref, own, sibling, *outs):
    mine = pl.program_id(0) == 0

    def write(block):
        segs, rows, width = block.shape
        if turned:
            outs[0][...] = block[...].reshape(segs * rows, width).astype(F32).T
            return
        unit = sum(parts)
        for s in range(segs):
            tile = block[s].astype(F32)
            start = 0
            for out, part in zip(outs, parts):
                for u in range(width // unit):
                    out[s * rows : (s + 1) * rows, u * part : (u + 1) * part] = tile[
                        :, u * unit + start : u * unit + start + part
                    ]
                start += part

    @pl.when(mine)
    def _():
        write(own)

    @pl.when(jnp.logical_not(mine))
    def _():
        write(sibling)


def unpack(own, sibling, place, first, blocks, rows, parts, cores):
    segs, _, width = own.shape
    unit = sum(parts)
    if width % unit or rows % 16 or cores != 2:
        total = segs * rows
        full = jnp.zeros((total, cores * blocks * width), BF16)
        for c, source in enumerate([own, sibling][:cores]):
            for b in range(blocks):
                start = (first + b) * rows
                piece = source[:, start : start + rows].reshape(total, width)
                full = lax.dynamic_update_slice(full, piece, (0, place[c * blocks + b] * width))
        outs, start = [], 0
        for part in parts:
            outs.append(
                jnp.concatenate(
                    [full[:, i + start : i + start + part] for i in range(0, full.shape[1], unit)],
                    axis=1,
                ).astype(F32)
            )
            start += part
        return outs
    units = width // unit
    batch = segs // 2

    def source(which):
        def index(c, b, k, place_ref):
            here = c == which
            fixed_b, fixed_k = (blocks - 1, 1) if which == 0 else (0, 0)
            return jnp.where(here, k, fixed_k), first + jnp.where(here, b, fixed_b), 0

        return index

    def target(c, b, k, place_ref):
        return k, place_ref[c * blocks + b]

    return pl.pallas_call(
        functools.partial(unpack_kernel, parts, False),
        grid_spec=pltpu.PrefetchScalarGridSpec(
            num_scalar_prefetch=1,
            grid=(cores, blocks, 2),
            in_specs=[
                pl.BlockSpec((batch, rows, width), source(0)),
                pl.BlockSpec((batch, rows, width), source(1)),
            ],
            out_specs=[pl.BlockSpec((batch * rows, units * part), target) for part in parts],
        ),
        out_shape=[
            jax.ShapeDtypeStruct((segs * rows, cores * blocks * units * part), F32)
            for part in parts
        ],
        name="unpack",
    )(place, own, sibling)


def unpack_rows(own, sibling, core, first, rows, turned, cores):
    segs, total, width = own.shape
    if first % rows or rows % 16 or cores != 2:
        pieces = [v[:, first : first + rows].reshape(segs * rows, width) for v in (own, sibling)]
        both = pieces[0]
        if cores > 1:
            both = jnp.where(
                core == 0, jnp.concatenate(pieces), jnp.concatenate(pieces[::-1])
            )
        return (both.T if turned else both).astype(F32)
    batch = segs // 2

    def source(which):
        def index(c, k, place_ref):
            return jnp.where(c == which, k, 1 - which), first // rows, 0

        return index

    def target(c, k, place_ref):
        at = place_ref[c] * 2 + k
        return (0, at) if turned else (at, 0)

    tall = cores * segs * rows
    return pl.pallas_call(
        functools.partial(unpack_kernel, (width,), turned),
        grid_spec=pltpu.PrefetchScalarGridSpec(
            num_scalar_prefetch=1,
            grid=(cores, 2),
            in_specs=[
                pl.BlockSpec((batch, rows, width), source(0)),
                pl.BlockSpec((batch, rows, width), source(1)),
            ],
            out_specs=pl.BlockSpec(
                (width, batch * rows) if turned else (batch * rows, width), target
            ),
        ),
        out_shape=jax.ShapeDtypeStruct((width, tall) if turned else (tall, width), F32),
        name="unpack_rows",
    )(jnp.stack([core, 1 - core]).astype(jnp.int32), own, sibling)


def chip_cycle(mesh):
    column = mesh.devices.reshape(mesh.shape["replica"], mesh.shape["fsdp"])[:, 0]
    total = len(column)
    coords = [tuple(getattr(d, "coords", None) or ()) for d in column]
    cores = 1
    if all(coords):
        while cores < total and coords[cores] == coords[0]:
            cores += 1
    chips = coords[::cores]
    count = len(chips)
    order = list(range(count))
    if count * cores == total and len(set(chips)) == count and all(chips):
        varying = [a for a in range(3) if len({c[a] for c in chips}) > 1]
        if len(varying) == 2:
            values = [sorted({c[a] for c in chips}) for a in varying]
            place = {
                tuple(values[i].index(c[a]) for i, a in enumerate(varying)): k
                for k, c in enumerate(chips)
            }
            high, wide = len(values[0]), len(values[1])
            if high * wide == count:
                if high % 2:
                    place = {(b, a): k for (a, b), k in place.items()}
                    high, wide = wide, high
                if high % 2 == 0:
                    walk = []
                    for row in range(high):
                        cols = range(1, wide) if row % 2 == 0 else range(wide - 1, 0, -1)
                        walk += [(row, col) for col in cols]
                    walk += [(row, 0) for row in range(high - 1, -1, -1)]
                    order = [place[w] for w in walk]
    return cores, order


class Links:
    def __init__(self, mesh):
        self.ranks = mesh.shape["fsdp"]
        self.replicas = mesh.shape["replica"]
        self.cores, self.cycle = chip_cycle(mesh)
        self.chips = len(self.cycle)
        table = np.zeros((self.chips,), np.int32)
        for place, chip in enumerate(self.cycle):
            table[chip] = place
        self.table = table

    def start(self):
        self.rank = lax.axis_index("fsdp")
        replica = lax.axis_index("replica")
        self.core = replica % self.cores
        self.place = jnp.asarray(self.table)[replica // self.cores]

    def from_rank(self, value, shift):
        pairs = [(i, (i - shift) % self.ranks) for i in range(self.ranks)]
        return lax.ppermute(value, "fsdp", pairs)

    def others(self, value):
        return [self.from_rank(value, s) for s in range(1, self.ranks)]

    def sibling(self, value):
        pairs = [
            (chip * self.cores + core, chip * self.cores + (core + 1) % self.cores)
            for chip in range(self.chips)
            for core in range(self.cores)
        ]
        return lax.ppermute(value, "replica", pairs)

    def along(self, value, direction):
        pairs = [
            (
                self.cycle[i] * self.cores + core,
                self.cycle[(i + direction) % self.chips] * self.cores + core,
            )
            for i in range(self.chips)
            for core in range(self.cores)
        ]
        return lax.ppermute(value, "replica", pairs)

    def total(self, value):
        for axis, size in (("replica", self.replicas), ("fsdp", self.ranks)):
            if size & (size - 1):
                value = lax.psum(value, axis)
                continue
            step = 1
            while step < size:
                value = value + lax.ppermute(value, axis, [(i, i ^ step) for i in range(size)])
                step *= 2
        return value

    def reduce(self, grad, spread, hooks=()):
        chips = self.chips
        starts = [self.place, (chips - self.place) % chips]

        def at(turn, index):
            return turn * chips + lax.rem(index + 2 * chips, chips)

        def local(turn, index):
            return lax.dynamic_index_in_dim(grad, at(turn, index), 0, keepdims=False)

        held = [local(t, q) for t, q in enumerate(starts)]
        for step in range(chips - 1):
            with jax.named_scope(f"reduce_{step}"):
                for t, direction in enumerate((1, -1)):
                    got = self.along(held[t], direction).astype(F32)
                    held[t] = (got + local(t, starts[t] - step - 1).astype(F32)).astype(BF16)
        held = [self.swap(h, spread) for h in held]
        result = jnp.zeros(grad.shape, BF16)
        for t, q in enumerate(starts):
            result = lax.dynamic_update_index_in_dim(result, held[t], at(t, q + 1), 0)
        for step in range(chips - 1):
            with jax.named_scope(f"gather_{step}"):
                if step in hooks:
                    held = hooks[step](held)
                for t, direction in enumerate((1, -1)):
                    held[t] = self.along(held[t], direction)
                    result = lax.dynamic_update_index_in_dim(
                        result, held[t], at(t, starts[t] - step), 0
                    )
        return result

    def swap(self, value, spread):
        size = spread // self.ranks
        pieces = [lax.dynamic_slice_in_dim(value, self.rank * size, size, 0)]
        for s in range(1, self.ranks):
            to = (self.rank - s + self.ranks) % self.ranks
            pieces.append(self.from_rank(lax.dynamic_slice_in_dim(value, to * size, size, 0), s))
        return jnp.concatenate(pieces + [value[spread:]], axis=0)


def shards(
    links,
    block_in,
    w_query,
    key_projection,
    value_projection,
    w_out,
    w_gate,
    w_up,
    w_down,
    attn_gain,
    mlp_gain,
    query_gain,
    key_norm_gain,
    segment_ids,
    positions,
    cotangent,
):
    links.start()
    ranks, cores = links.ranks, links.cores
    rank, core = links.rank, links.core
    tokens, width = block_in.shape
    sequence = tokens * ranks
    segment_row = segment_ids[0]

    hidden_units = w_down.shape[0]
    unit = 256 if hidden_units % 512 == 0 else 128
    qkv_units = (GROUP * HEAD_SIZE, HEAD_SIZE, HEAD_SIZE)

    def column_block(arrays, units, after):
        rows = arrays[0].shape[0]
        half = rows // cores
        pieces, places = [], []
        for s in range(1, ranks):
            to = (rank - s + ranks) % ranks
            sent = pack(arrays, units, to, ranks, half, core, 0 * core, half)
            if after is not None:
                sent, _ = lax.optimization_barrier((sent, after))
            piece = links.from_rank(sent, s)
            base = ((rank + s) % ranks) * cores
            held = core
            for turn in range(cores):
                pieces.append(piece)
                places.append(base + held)
                if turn + 1 < cores:
                    piece = links.sibling(piece)
                    held = (held - 1 + cores) % cores
        full = pack(arrays, units, rank, ranks, rows, 0 * rank, rank, rows * ranks)
        return insert(full, pieces, places)

    rows_in = jnp.concatenate([block_in] + links.others(block_in), axis=0)
    position_row = jnp.concatenate([positions] + links.others(positions), axis=0)
    w_qkv = column_block((w_query, key_projection, value_projection), qkv_units, None)
    cot = jnp.concatenate([cotangent] + links.others(cotangent), axis=0)
    w_gu = column_block((w_gate, w_up), (unit, unit), rows_in[:8, :128])

    offset = rank * tokens
    token = lax.rem(offset + jnp.arange(sequence, dtype=jnp.int32), sequence)
    segments = lax.dynamic_slice_in_dim(
        jnp.concatenate([segment_row, segment_row]), offset, sequence
    )
    mask = (
        (token[None, :] <= token[:, None]) & (segments[None, :] == segments[:, None])
    ).astype(F32)
    cos_tab, sin_tab = rope_tables(position_row, HEAD_SIZE)
    q_gain, k_gain = query_gain[None, :], key_norm_gain[None, :]

    resid = rows_in.astype(F32)
    scale_one = inv_rms(resid)
    normed = (resid * scale_one * attn_gain).astype(BF16)
    attn_out, qkv = attention(normed, w_qkv, cos_tab, sin_tab, mask, q_gain, k_gain)
    mid_part = dot_nn(attn_out, w_out)

    def all_summed(part):
        total = part
        sent = part.astype(BF16)
        for s in range(1, ranks):
            got = links.from_rank(sent, s)
            total = total + jnp.roll(got, s * tokens, axis=0).astype(F32)
        return total

    def own_summed(part):
        total = part[:tokens]
        for s in range(1, ranks):
            far = (ranks - s) * tokens
            total = total + links.from_rank(part[far : far + tokens].astype(BF16), s).astype(F32)
        return total

    mid = resid + all_summed(mid_part)
    scale_two = inv_rms(mid)
    normed_two = (mid * scale_two * mlp_gain).astype(BF16)
    hidden, d_gu, d_normed_part, down_part = mlp(normed_two, cot, w_gu, w_down, unit)

    d_normed_two = all_summed(d_normed_part)

    def both(value):
        return jnp.concatenate([value, links.sibling(value)], axis=0) if cores > 1 else value

    def both_of_columns(value):
        size = value.shape[1] // cores
        own = lax.dynamic_slice_in_dim(value, core * size, size, 1)
        if cores == 1:
            return own
        theirs = lax.dynamic_slice_in_dim(value, ((core + 1) % cores) * size, size, 1)
        return jnp.concatenate([own, links.sibling(theirs)], axis=0)

    segs = 2 * links.chips

    def segments_of(spread, plain):
        wide = spread.shape[1]
        first = spread.reshape(ranks, segs, -1, wide).transpose(1, 0, 2, 3).reshape(segs, -1, wide)
        return jnp.concatenate([first, plain.reshape(segs, -1, wide)], axis=1), first.shape[1]

    def product(rows_of, columns_of):
        return dot_tn(both_of_columns(rows_of), both(columns_of), BF16)

    grad_gu = dot_tn(both(normed_two), both_of_columns(d_gu), BF16)
    turn_down = grad_gu.shape[1] != width
    grad_down = product(cot, hidden) if turn_down else product(hidden, cot)
    mlp_grads, mlp_spread = segments_of(grad_gu, grad_down)
    sum_mlp = links.reduce(mlp_grads, mlp_spread)

    grad_mlp_gain = jnp.sum((d_normed_two * mid * scale_two)[:tokens], axis=0)
    d_mid = cot.astype(F32) + norm_backward(d_normed_two, mid, scale_two, mlp_gain)
    d_mid_b = d_mid.astype(BF16)
    d_attn = dot_nt(d_mid_b, w_out).astype(BF16)
    d_qkv, d_q_gain, d_k_gain = attention_back(
        qkv, cos_tab, sin_tab, mask, q_gain, k_gain, d_attn
    )
    grad_qkv = dot_tn(both(normed), both_of_columns(d_qkv), BF16)
    turn_out = grad_qkv.shape[1] != width
    grad_out = product(d_mid_b, attn_out) if turn_out else product(attn_out, d_mid_b)
    attn_grads, attn_spread = segments_of(grad_qkv, grad_out)

    d_normed = own_summed(dot_nt(d_qkv, w_qkv))
    resid_own, scale_own = resid[:tokens], scale_one[:tokens]
    grad_attn_gain = jnp.sum(d_normed * resid_own * scale_own, axis=0)
    d_block_in = d_mid[:tokens] + norm_backward(d_normed, resid_own, scale_own, attn_gain)
    block_out = (mid[:tokens] + own_summed(down_part)).astype(BF16)

    gains = links.total(
        jnp.concatenate(
            [
                grad_attn_gain,
                grad_mlp_gain,
                jnp.sum(d_q_gain, axis=(0, 1)),
                jnp.sum(d_k_gain, axis=(0, 1)),
            ]
        ).reshape(-1, HEAD_SIZE)
    ).reshape(-1)

    turns = (core + jnp.arange(cores, dtype=jnp.int32)) % cores
    origin = (rank + jnp.arange(ranks, dtype=jnp.int32)) % ranks
    place = (origin[None, :] * cores + turns[:, None]).reshape(-1)

    def spread_out(summed, spread, parts, turned):
        other = links.sibling(summed) if cores > 1 else summed
        size = spread // ranks
        split = unpack(summed, other, place, 0, ranks, size, parts, cores)
        plain = unpack_rows(
            summed, other, core, spread, summed.shape[1] - spread, turned, cores
        )
        return split, plain

    def with_gains(held):
        nonlocal gains
        held[0], gains = lax.optimization_barrier((held[0], gains))
        return held

    sum_attn = links.reduce(attn_grads, attn_spread, {0: with_gains})
    (total_gate, total_up), total_down = spread_out(sum_mlp, mlp_spread, (unit, unit), turn_down)
    (total_query, total_key, total_value), total_out = spread_out(
        sum_attn, attn_spread, qkv_units, turn_out
    )
    return (
        block_out,
        d_block_in,
        total_query,
        total_key,
        total_value,
        total_out,
        total_gate,
        total_up,
        total_down,
        gains[:width],
        gains[width : 2 * width],
        gains[2 * width : 2 * width + HEAD_SIZE],
        gains[2 * width + HEAD_SIZE :],
    )


def solution(mesh):
    rows = P(("replica", "fsdp"), None)
    weight = P("fsdp", None)
    in_specs = (
        (rows,)
        + (weight,) * 7
        + (P(),) * 4
        + (P("replica", None), P(("replica", "fsdp")), rows)
    )
    out_specs = (rows, rows) + (weight,) * 7 + (P(),) * 4
    return jax.shard_map(
        functools.partial(shards, Links(mesh)),
        mesh=mesh,
        in_specs=in_specs,
        out_specs=out_specs,
        check_vma=False,
    )
```

```python
import functools

import jax
import jax.numpy as jnp
import numpy as np
from jax import lax
from jax.experimental import pallas as pl
from jax.experimental.pallas import tpu as pltpu
from jax.sharding import PartitionSpec as P

QUERY_HEADS = 16
KEY_VALUE_HEADS = 8
HEAD_SIZE = 128
GROUP = QUERY_HEADS // KEY_VALUE_HEADS

EPS = 1e-06
THETA = 1000000.0
NEG = -1e30


F32 = jnp.float32
BF16 = jnp.bfloat16


def inv_rms(value):
    return lax.rsqrt(jnp.mean(value * value, axis=-1, keepdims=True) + EPS)


def norm_backward(grad, value, scale, gain):
    upstream = grad * gain
    return scale * (
        upstream - value * scale * scale * jnp.mean(upstream * value, axis=-1, keepdims=True)
    )


def dot_nn(left, right):
    return lax.dot_general(left, right, (((1,), (0,)), ((), ())), preferred_element_type=F32)


def dot_nt(left, right):
    return lax.dot_general(left, right, (((1,), (1,)), ((), ())), preferred_element_type=F32)


def dot_tn(left, right, dtype=F32):
    return lax.dot_general(left, right, (((0,), (0,)), ((), ())), preferred_element_type=dtype)


def rope_tables(position_row, width):
    half = width // 2
    freq = jnp.exp(
        -(jnp.arange(half, dtype=F32) * (2.0 / width)) * jnp.log(jnp.float32(THETA))
    )
    angle = position_row.astype(F32)[:, None] * freq[None, :]
    cos, sin = jnp.cos(angle), jnp.sin(angle)
    return jnp.concatenate([cos, cos], axis=-1), jnp.concatenate([-sin, sin], axis=-1)


def _half_turn(value):
    return pltpu.roll(value, HEAD_SIZE // 2, axis=1)


def _rotated(raw, gain, cos, sin):
    scale = inv_rms(raw)
    normed = raw * scale * gain
    return (normed * cos + _half_turn(normed) * sin).astype(BF16), scale


def _probs(q_rot, k_rot, mask):
    scores = dot_nt(q_rot, k_rot) * HEAD_SIZE ** (-0.5)
    scores = jnp.where(mask > 0.5, scores, NEG)
    top = jnp.max(scores, axis=-1, keepdims=True)
    lse = top + jnp.log(jnp.sum(jnp.exp(scores - top), axis=-1, keepdims=True))
    return jnp.exp(scores - lse)


def _head(index):
    return pl.ds(index * HEAD_SIZE, HEAD_SIZE)


def _row_chunks(rows, body):
    chunk = min(rows, 256)
    if rows == chunk:
        body(pl.ds(0, rows))
    else:

        def step(i, carry):
            body(pl.ds(pl.multiple_of(i * chunk, chunk), chunk))
            return carry

        lax.fori_loop(0, rows // chunk, step, 0)


def _columns(offsets, index, size):
    return pl.ds(pl.multiple_of(offsets[index], 128), size)


def _piecewise(left, rows, offsets, pieces):
    total = None
    for i, piece in enumerate(pieces):
        part = dot_nn(left[rows, _columns(offsets, i, piece.shape[0])], piece[...])
        total = part if total is None else total + part
    return total


def attention_kernel(count, offsets, normed, *refs):
    pieces = refs[:count]
    cos, sin, mask, q_gain, k_gain, out, qkv, k_scr, v_scr = refs[count:]

    def project(rows):
        block = _piecewise(normed, rows, offsets, pieces)
        qkv[rows, :] = block
        k_raw = block[:, GROUP * HEAD_SIZE : (GROUP + 1) * HEAD_SIZE]
        k_scr[rows, :], _ = _rotated(k_raw, k_gain[...], cos[rows, :], sin[rows, :])
        v_scr[rows, :] = block[:, (GROUP + 1) * HEAD_SIZE :].astype(BF16)

    def attend(rows):
        for h in range(GROUP):
            q_rot, _ = _rotated(qkv[rows, _head(h)], q_gain[...], cos[rows, :], sin[rows, :])
            probs = _probs(q_rot, k_scr[...], mask[rows, :]).astype(BF16)
            out[rows, _head(h)] = dot_nn(probs, v_scr[...]).astype(BF16)

    _row_chunks(normed.shape[0], project)
    _row_chunks(normed.shape[0], attend)


def attention_back_kernel(
    qkv, cos, sin, mask, q_gain, k_gain, d_attn, d_qkv, d_q_gain, d_k_gain, k_scr, v_scr, dk_scr, dv_scr
):
    total = qkv.shape[0]

    def prepare(rows):
        k_scr[rows, :], _ = _rotated(qkv[rows, _head(GROUP)], k_gain[...], cos[rows, :], sin[rows, :])
        v_scr[rows, :] = qkv[rows, _head(GROUP + 1)].astype(BF16)
        dk_scr[rows, :] = jnp.zeros((rows.size, HEAD_SIZE), F32)
        dv_scr[rows, :] = jnp.zeros((rows.size, HEAD_SIZE), F32)

    def queries(rows):
        for h in range(GROUP):
            q_raw = qkv[rows, _head(h)]
            q_rot, q_scale = _rotated(q_raw, q_gain[...], cos[rows, :], sin[rows, :])
            probs = _probs(q_rot, k_scr[...], mask[rows, :])
            grad = d_attn[rows, _head(h)]
            d_prob = dot_nt(grad, v_scr[...])
            d_scores = (
                probs
                * (d_prob - jnp.sum(probs * d_prob, axis=-1, keepdims=True))
                * HEAD_SIZE ** (-0.5)
            ).astype(BF16)
            d_q = dot_nn(d_scores, k_scr[...])
            dk_scr[...] += dot_tn(d_scores, q_rot)
            dv_scr[...] += dot_tn(probs.astype(BF16), grad)
            d_normed = d_q * cos[rows, :] - _half_turn(d_q) * sin[rows, :]
            d_q_gain[0] += jnp.sum(d_normed * q_raw * q_scale, axis=0, keepdims=True)
            d_qkv[rows, _head(h)] = norm_backward(d_normed, q_raw, q_scale, q_gain[...]).astype(BF16)

    def keys(rows):
        k_raw = qkv[rows, _head(GROUP)]
        k_scale = inv_rms(k_raw)
        d_k = dk_scr[rows, :]
        d_normed = d_k * cos[rows, :] - _half_turn(d_k) * sin[rows, :]
        d_k_gain[0] += jnp.sum(d_normed * k_raw * k_scale, axis=0, keepdims=True)
        d_qkv[rows, _head(GROUP)] = norm_backward(d_normed, k_raw, k_scale, k_gain[...]).astype(BF16)
        d_qkv[rows, _head(GROUP + 1)] = dv_scr[rows, :].astype(BF16)

    d_q_gain[...] = jnp.zeros(d_q_gain.shape, F32)
    d_k_gain[...] = jnp.zeros(d_k_gain.shape, F32)
    _row_chunks(total, prepare)
    _row_chunks(total, queries)
    _row_chunks(total, keys)


def _whole(shape):
    return pl.BlockSpec(shape, lambda *g: (0,) * len(shape))


def attention(normed, pieces, offsets, cos, sin, mask, q_gain, k_gain):
    tokens, _ = normed.shape
    width = pieces[0].shape[1]
    packed = (GROUP + 2) * HEAD_SIZE
    groups = width // packed
    return pl.pallas_call(
        functools.partial(attention_kernel, len(pieces)),
        grid_spec=pltpu.PrefetchScalarGridSpec(
            num_scalar_prefetch=1,
            grid=(groups,),
            in_specs=[
                _whole(normed.shape),
                *[pl.BlockSpec((p.shape[0], packed), lambda g, _: (0, g)) for p in pieces],
                _whole(cos.shape),
                _whole(sin.shape),
                _whole(mask.shape),
                _whole(q_gain.shape),
                _whole(k_gain.shape),
            ],
            out_specs=[
                pl.BlockSpec((tokens, GROUP * HEAD_SIZE), lambda g, _: (0, g)),
                pl.BlockSpec((tokens, packed), lambda g, _: (0, g)),
            ],
            scratch_shapes=[pltpu.VMEM((tokens, HEAD_SIZE), BF16)] * 2,
        ),
        out_shape=[
            jax.ShapeDtypeStruct((tokens, groups * GROUP * HEAD_SIZE), BF16),
            jax.ShapeDtypeStruct((tokens, width), F32),
        ],
        name="attention",
    )(offsets, normed, *pieces, cos, sin, mask, q_gain, k_gain)


def attention_back(qkv, cos, sin, mask, q_gain, k_gain, d_attn):
    tokens, width = qkv.shape
    packed = (GROUP + 2) * HEAD_SIZE
    groups = width // packed
    return pl.pallas_call(
        attention_back_kernel,
        grid=(groups,),
        in_specs=[
            pl.BlockSpec((tokens, packed), lambda g: (0, g)),
            _whole(cos.shape),
            _whole(sin.shape),
            _whole(mask.shape),
            _whole(q_gain.shape),
            _whole(k_gain.shape),
            pl.BlockSpec((tokens, GROUP * HEAD_SIZE), lambda g: (0, g)),
        ],
        out_specs=[
            pl.BlockSpec((tokens, packed), lambda g: (0, g)),
            pl.BlockSpec((1, 1, HEAD_SIZE), lambda g: (g, 0, 0)),
            pl.BlockSpec((1, 1, HEAD_SIZE), lambda g: (g, 0, 0)),
        ],
        out_shape=[
            jax.ShapeDtypeStruct((tokens, width), BF16),
            jax.ShapeDtypeStruct((groups, 1, HEAD_SIZE), F32),
            jax.ShapeDtypeStruct((groups, 1, HEAD_SIZE), F32),
        ],
        scratch_shapes=[pltpu.VMEM((tokens, HEAD_SIZE), BF16)] * 2
        + [pltpu.VMEM((tokens, HEAD_SIZE), F32)] * 2,
        name="attention_back",
    )(qkv, cos, sin, mask, q_gain, k_gain, d_attn)


def mlp_kernel(count, offsets, normed, cotangent, *refs):
    pieces = refs[:count]
    w_down, hidden, d_gu, d_normed, down = refs[count:]
    unit = w_down.shape[0]

    @pl.when(pl.program_id(0) == 0)
    def _():
        d_normed[...] = jnp.zeros(d_normed.shape, F32)
        down[...] = jnp.zeros(down.shape, F32)

    gate_up = _piecewise(normed, slice(None), offsets, pieces)
    gate, up = gate_up[:, :unit], gate_up[:, unit:]
    d_hidden = dot_nt(cotangent[...], w_down[...])
    sig = jax.nn.sigmoid(gate)
    hid = (gate * sig * up).astype(BF16)
    hidden[...] = hid
    d_gu[:, :unit] = (d_hidden * up * sig * (1.0 + gate * (1.0 - sig))).astype(BF16)
    d_gu[:, unit:] = (d_hidden * gate * sig).astype(BF16)
    for i, piece in enumerate(pieces):
        d_normed[:, _columns(offsets, i, piece.shape[0])] += dot_nt(d_gu[...], piece[...])
    down[...] += dot_nn(hid, w_down[...])


def mlp(normed, cotangent, pieces, offsets, w_down, unit):
    tokens, width = normed.shape
    ff = w_down.shape[0]
    return pl.pallas_call(
        functools.partial(mlp_kernel, len(pieces)),
        grid_spec=pltpu.PrefetchScalarGridSpec(
            num_scalar_prefetch=1,
            grid=(ff // unit,),
            in_specs=[
                _whole(normed.shape),
                _whole(cotangent.shape),
                *[pl.BlockSpec((p.shape[0], 2 * unit), lambda g, _: (0, g)) for p in pieces],
                pl.BlockSpec((unit, width), lambda g, _: (g, 0)),
            ],
            out_specs=[
                pl.BlockSpec((tokens, unit), lambda g, _: (0, g)),
                pl.BlockSpec((tokens, 2 * unit), lambda g, _: (0, g)),
                _whole((tokens, width)),
                _whole((tokens, width)),
            ],
        ),
        out_shape=[
            jax.ShapeDtypeStruct((tokens, ff), BF16),
            jax.ShapeDtypeStruct((tokens, 2 * ff), BF16),
            jax.ShapeDtypeStruct((tokens, width), F32),
            jax.ShapeDtypeStruct((tokens, width), F32),
        ],
        name="mlp",
    )(offsets, normed, cotangent, *pieces, w_down)


def back_project_kernel(count, offsets, grad, *refs):
    pieces, out = refs[:count], refs[count]

    @pl.when(pl.program_id(0) == 0)
    def _():
        out[...] = jnp.zeros(out.shape, F32)

    for i, piece in enumerate(pieces):
        out[:, _columns(offsets, i, piece.shape[0])] += dot_nt(grad[...], piece[...])


def back_project(grad, pieces, offsets, width):
    tokens, wide = grad.shape
    block = min(wide, 1024)
    return pl.pallas_call(
        functools.partial(back_project_kernel, len(pieces)),
        grid_spec=pltpu.PrefetchScalarGridSpec(
            num_scalar_prefetch=1,
            grid=(wide // block,),
            in_specs=[
                pl.BlockSpec((tokens, block), lambda g, _: (0, g)),
                *[pl.BlockSpec((p.shape[0], block), lambda g, _: (0, g)) for p in pieces],
            ],
            out_specs=_whole((tokens, width)),
        ),
        out_shape=jax.ShapeDtypeStruct((tokens, width), F32),
        name="back_project",
    )(offsets, grad, *pieces)


def pack_kernel(units, place_ref, *refs):
    arrays, out = refs[:-1], refs[-1]
    start = 0
    for i in range(arrays[0].shape[1] // units[0]):
        for a, u in zip(arrays, units):
            out[:, start : start + u] = a[:, i * u : (i + 1) * u]
            start += u


def pack(arrays, units, column, count, rows, from_row):
    steps = arrays[0].shape[1] // count // units[0]
    batch = next(b for b in (3, 2, 1) if steps % b == 0)
    place = jnp.stack([column * (steps // batch), from_row]).astype(jnp.int32)
    unit = sum(units)
    return pl.pallas_call(
        functools.partial(pack_kernel, units),
        grid_spec=pltpu.PrefetchScalarGridSpec(
            num_scalar_prefetch=1,
            grid=(steps // batch,),
            in_specs=[
                pl.BlockSpec((rows, batch * u), lambda i, place: (place[1], place[0] + i))
                for u in units
            ],
            out_specs=pl.BlockSpec((rows, batch * unit), lambda i, place: (0, i)),
        ),
        out_shape=jax.ShapeDtypeStruct((rows, steps * unit), BF16),
        name="pack",
    )(place, *arrays)


class Layout:
    def __init__(self, ranks, segs, width, gu, qkv, down_rows, out_rows):
        self.ranks, self.segs, self.width = ranks, segs, width
        self.gu, self.qkv = gu, qkv
        self.unit = int(np.gcd.reduce([gu, qkv, width]))
        self.seg = width // ranks // segs
        self.down_seg, self.out_seg = down_rows // segs, out_rows // segs
        self.spread = ranks * (gu + qkv) // self.unit * self.seg
        self.plain = (self.down_seg + self.out_seg) * width // self.unit

    def join(self, gu, qkv, down, out):
        def spread(grad):
            units = grad.shape[1] // self.unit
            split = grad.reshape(self.ranks, self.segs, self.seg, units, self.unit)
            split = split.transpose(1, 0, 3, 2, 4)
            return split.reshape(self.segs, self.ranks, units * self.seg, self.unit)

        def plain(grad):
            split = grad.reshape(self.segs, -1, self.width // self.unit, self.unit)
            return split.transpose(0, 2, 1, 3).reshape(self.segs, -1, self.unit)

        first = jnp.concatenate([spread(gu), spread(qkv)], axis=2)
        first = first.reshape(self.segs, self.spread, self.unit)
        return jnp.concatenate([first, plain(down), plain(out)], axis=1)

    def split(self, joined):
        first = joined[:, : self.spread].reshape(self.segs, self.ranks, -1, self.seg, self.unit)
        first = first.transpose(1, 0, 3, 2, 4).reshape(self.ranks, self.segs * self.seg, -1)

        def plain(part):
            split = part.reshape(self.segs, self.width // self.unit, -1, self.unit)
            return split.transpose(0, 2, 1, 3).reshape(-1, self.width)

        middle = self.spread + self.down_seg * self.width // self.unit
        return (
            first[:, :, : self.gu],
            first[:, :, self.gu :],
            plain(joined[:, self.spread : middle]),
            plain(joined[:, middle:]),
        )

    def aligned(self):
        return not (self.seg % 16 or self.down_seg % 16 or self.out_seg % 16 or self.unit % 512)


def deliver_kernel(layout, parts, cores, count, place, *refs):
    segments = refs[:count]
    tail = refs[-(2 * 7 + 1) :]
    outs, scratch, sems = tail[:7], tail[7:14], tail[14]
    lay = layout
    pending = []
    for k, segment in enumerate(segments):
        core, seg = place[3 * k], place[3 * k + 1]
        row = pl.multiple_of(seg * lay.seg, 16)

        def put(out, buffer, at_row, at_column):
            rows, columns = buffer.shape
            copy = pltpu.make_async_copy(
                buffer,
                out.at[pl.ds(at_row, rows), pl.ds(at_column, columns)],
                sems.at[len(pending)],
            )
            copy.start()
            pending.append(copy)

        start = 0
        for b in range(lay.ranks):
            block = place[3 * count + b] * cores + core
            index = 0
            for group, columns in ((parts[0], lay.gu), (parts[1], lay.qkv)):
                for u in range(columns // lay.unit):
                    value = segment[start : start + lay.seg, :].astype(F32)
                    start += lay.seg
                    left = 0
                    for p, part in enumerate(group):
                        scratch[index + p][k * lay.ranks + b, :, u * part : (u + 1) * part] = value[
                            :, left : left + part
                        ]
                        left += part
                for p in range(len(group)):
                    buffer = scratch[index + p].at[k * lay.ranks + b]
                    put(
                        outs[index + p],
                        buffer,
                        row,
                        pl.multiple_of(block * buffer.shape[1], 128),
                    )
                index += len(group)
        for index, rows in ((5, lay.down_seg), (6, lay.out_seg)):
            for u in range(lay.width // lay.unit):
                scratch[index][k, :, u * lay.unit : (u + 1) * lay.unit] = segment[
                    start : start + rows, :
                ].astype(F32)
                start += rows
            put(
                outs[index],
                scratch[index].at[k],
                pl.multiple_of((core * lay.segs + seg) * rows, 16),
                0,
            )
    for copy in pending:
        copy.wait()


def deliver(layout, parts, cores, segments, place, shapes, before):
    count = len(segments)
    lay = layout
    anywhere = pl.BlockSpec(memory_space=pl.ANY)
    widths = [lay.gu // sum(parts[0]) * p for p in parts[0]]
    widths += [lay.qkv // sum(parts[1]) * p for p in parts[1]]
    scratch = [pltpu.VMEM((count * lay.ranks, lay.seg, w), F32) for w in widths]
    scratch += [pltpu.VMEM((count, r, lay.width), F32) for r in (lay.down_seg, lay.out_seg)]
    copies = count * (lay.ranks * len(widths) + 2)
    rows = lay.spread + lay.plain
    before = [] if before is None else list(before)
    return pl.pallas_call(
        functools.partial(deliver_kernel, layout, parts, cores, count),
        grid_spec=pltpu.PrefetchScalarGridSpec(
            num_scalar_prefetch=1,
            grid=(1,),
            in_specs=[_whole((rows, lay.unit))] * count + [anywhere] * len(before),
            out_specs=[anywhere] * len(shapes),
            scratch_shapes=scratch + [pltpu.SemaphoreType.DMA((copies,))],
        ),
        out_shape=[jax.ShapeDtypeStruct(shape, F32) for shape in shapes],
        input_output_aliases={1 + count + i: i for i in range(len(before))},
        name="deliver",
    )(place, *segments, *before)


def split_columns(full, parts):
    unit, start, outs = sum(parts), 0, []
    for part in parts:
        pieces = [full[:, i + start : i + start + part] for i in range(0, full.shape[1], unit)]
        outs.append(jnp.concatenate(pieces, axis=1).astype(F32))
        start += part
    return outs


def chip_cycle(mesh):
    column = mesh.devices.reshape(mesh.shape["replica"], mesh.shape["fsdp"])[:, 0]
    total = len(column)
    coords = [tuple(getattr(d, "coords", None) or ()) for d in column]
    cores = 1
    if all(coords):
        while cores < total and coords[cores] == coords[0]:
            cores += 1
    chips = coords[::cores]
    count = len(chips)
    order = list(range(count))
    if count * cores == total and len(set(chips)) == count and all(chips):
        varying = [a for a in range(3) if len({c[a] for c in chips}) > 1]
        if len(varying) == 2:
            values = [sorted({c[a] for c in chips}) for a in varying]
            place = {
                tuple(values[i].index(c[a]) for i, a in enumerate(varying)): k
                for k, c in enumerate(chips)
            }
            high, wide = len(values[0]), len(values[1])
            if high * wide == count:
                if high % 2:
                    place = {(b, a): k for (a, b), k in place.items()}
                    high, wide = wide, high
                if high % 2 == 0:
                    walk = []
                    for row in range(high):
                        cols = range(1, wide) if row % 2 == 0 else range(wide - 1, 0, -1)
                        walk += [(row, col) for col in cols]
                    walk += [(row, 0) for row in range(high - 1, -1, -1)]
                    order = [place[w] for w in walk]
    return cores, order


class Links:
    def __init__(self, mesh):
        self.ranks = mesh.shape["fsdp"]
        self.replicas = mesh.shape["replica"]
        self.cores, self.cycle = chip_cycle(mesh)
        self.chips = len(self.cycle)
        table = np.zeros((self.chips,), np.int32)
        for place, chip in enumerate(self.cycle):
            table[chip] = place
        self.table = table

    def start(self):
        self.rank = lax.axis_index("fsdp")
        replica = lax.axis_index("replica")
        self.core = replica % self.cores
        self.place = jnp.asarray(self.table)[replica // self.cores]

    def from_rank(self, value, shift):
        pairs = [(i, (i - shift) % self.ranks) for i in range(self.ranks)]
        return lax.ppermute(value, "fsdp", pairs)

    def others(self, value):
        return [self.from_rank(value, s) for s in range(1, self.ranks)]

    def sibling(self, value):
        pairs = [
            (chip * self.cores + core, chip * self.cores + (core + 1) % self.cores)
            for chip in range(self.chips)
            for core in range(self.cores)
        ]
        return lax.ppermute(value, "replica", pairs)

    def along(self, value, direction):
        pairs = [
            (
                self.cycle[i] * self.cores + core,
                self.cycle[(i + direction) % self.chips] * self.cores + core,
            )
            for i in range(self.chips)
            for core in range(self.cores)
        ]
        return lax.ppermute(value, "replica", pairs)

    def total(self, value):
        for axis, size in (("replica", self.replicas), ("fsdp", self.ranks)):
            if size & (size - 1):
                value = lax.psum(value, axis)
                continue
            step = 1
            while step < size:
                value = value + lax.ppermute(value, axis, [(i, i ^ step) for i in range(size)])
                step *= 2
        return value

    def reduce(self, grad, spread, take):
        chips = self.chips
        starts = [self.place, (chips - self.place) % chips]

        def at(turn, index):
            return turn * chips + lax.rem(index + 2 * chips, chips)

        def local(turn, index):
            return lax.dynamic_index_in_dim(grad, at(turn, index), 0, keepdims=False)

        held = [local(t, q) for t, q in enumerate(starts)]
        for step in range(chips - 1):
            for t, direction in enumerate((1, -1)):
                got = self.along(held[t], direction).astype(F32)
                held[t] = (got + local(t, starts[t] - step - 1).astype(F32)).astype(BF16)
        held = [self.swap(h, spread) for h in held]
        for step in range(chips):
            held = take(step, held, [at(t, q + 1 - step) for t, q in enumerate(starts)])
            if step < chips - 1:
                held = [self.along(h, d) for h, d in zip(held, (1, -1))]

    def swap(self, value, spread):
        size = spread // self.ranks
        pieces = [lax.dynamic_slice_in_dim(value, self.rank * size, size, 0)]
        for s in range(1, self.ranks):
            to = (self.rank - s + self.ranks) % self.ranks
            pieces.append(self.from_rank(lax.dynamic_slice_in_dim(value, to * size, size, 0), s))
        return jnp.concatenate(pieces + [value[spread:]], axis=0)


def shards(
    links,
    block_in,
    w_query,
    key_projection,
    value_projection,
    w_out,
    w_gate,
    w_up,
    w_down,
    attn_gain,
    mlp_gain,
    query_gain,
    key_norm_gain,
    segment_ids,
    positions,
    cotangent,
):
    links.start()
    ranks, cores = links.ranks, links.cores
    rank, core = links.rank, links.core
    tokens, width = block_in.shape
    sequence = tokens * ranks
    segment_row = segment_ids[0]

    hidden_units = w_down.shape[0]
    unit = 256 if hidden_units % 512 == 0 else 128
    qkv_units = (GROUP * HEAD_SIZE, HEAD_SIZE, HEAD_SIZE)

    def column_block(arrays, units, after):
        rows = arrays[0].shape[0]
        half = rows // cores
        pieces, places, came = [], [], None
        for s in range(1, ranks):
            to = (rank - s + ranks) % ranks
            sent = pack(arrays, units, to, ranks, half, core)
            if after is not None:
                sent, _ = lax.optimization_barrier((sent, after))
            piece = links.from_rank(sent, s)
            came = piece
            base = ((rank + s) % ranks) * rows
            held = core
            for turn in range(cores):
                pieces.append(piece)
                places.append(base + held * half)
                if turn + 1 < cores:
                    piece = links.sibling(piece)
                    held = (held - 1 + cores) % cores
        own = pack(arrays, units, rank, ranks, rows, 0 * rank)
        offsets = jnp.stack([rank * rows] + places).astype(jnp.int32)
        return [own] + pieces, offsets, came

    rows_in = jnp.concatenate([block_in] + links.others(block_in), axis=0)
    position_row = jnp.concatenate([positions] + links.others(positions), axis=0)
    w_qkv, at_qkv, came = column_block(
        (w_query, key_projection, value_projection), qkv_units, None
    )
    if came is None:
        came = rows_in
    far_cot, _ = lax.optimization_barrier((cotangent, came[:8, :128]))
    cot = jnp.concatenate([cotangent] + links.others(far_cot), axis=0)
    w_gu, at_gu, _ = column_block((w_gate, w_up), (unit, unit), came[:8, :128])

    offset = rank * tokens
    token = lax.rem(offset + jnp.arange(sequence, dtype=jnp.int32), sequence)
    segments = lax.dynamic_slice_in_dim(
        jnp.concatenate([segment_row, segment_row]), offset, sequence
    )
    mask = (
        (token[None, :] <= token[:, None]) & (segments[None, :] == segments[:, None])
    ).astype(F32)
    cos_tab, sin_tab = rope_tables(position_row, HEAD_SIZE)
    q_gain, k_gain = query_gain[None, :], key_norm_gain[None, :]

    resid = rows_in.astype(F32)
    scale_one = inv_rms(resid)
    normed = (resid * scale_one * attn_gain).astype(BF16)
    attn_out, qkv = attention(normed, w_qkv, at_qkv, cos_tab, sin_tab, mask, q_gain, k_gain)
    mid_part = dot_nn(attn_out, w_out)

    def all_summed(part):
        total = part
        sent = part.astype(BF16)
        for s in range(1, ranks):
            got = links.from_rank(sent, s)
            total = total + jnp.roll(got, s * tokens, axis=0).astype(F32)
        return total

    def own_summed(part):
        total = part[:tokens]
        for s in range(1, ranks):
            far = (ranks - s) * tokens
            total = total + links.from_rank(part[far : far + tokens].astype(BF16), s).astype(F32)
        return total

    mid = resid + all_summed(mid_part)
    scale_two = inv_rms(mid)
    normed_two = (mid * scale_two * mlp_gain).astype(BF16)
    hidden, d_gu, d_normed_part, down_part = mlp(normed_two, cot, w_gu, at_gu, w_down, unit)

    d_normed_two = all_summed(d_normed_part)

    def both(value):
        return jnp.concatenate([value, links.sibling(value)], axis=0) if cores > 1 else value

    def both_of_columns(value):
        size = value.shape[1] // cores
        own = lax.dynamic_slice_in_dim(value, core * size, size, 1)
        if cores == 1:
            return own
        theirs = lax.dynamic_slice_in_dim(value, ((core + 1) % cores) * size, size, 1)
        return jnp.concatenate([own, links.sibling(theirs)], axis=0)

    grad_gu = dot_tn(both(normed_two), both_of_columns(d_gu), BF16)
    grad_down = dot_tn(both_of_columns(hidden), both(cot), BF16)

    grad_mlp_gain = jnp.sum((d_normed_two * mid * scale_two)[:tokens], axis=0)
    d_mid = cot.astype(F32) + norm_backward(d_normed_two, mid, scale_two, mlp_gain)
    d_mid_b = d_mid.astype(BF16)
    d_attn = dot_nt(d_mid_b, w_out).astype(BF16)
    d_qkv, d_q_gain, d_k_gain = attention_back(
        qkv, cos_tab, sin_tab, mask, q_gain, k_gain, d_attn
    )
    grad_qkv = dot_tn(both(normed), both_of_columns(d_qkv), BF16)
    grad_out = dot_tn(both_of_columns(attn_out), both(d_mid_b), BF16)

    d_normed = own_summed(back_project(d_qkv, w_qkv, at_qkv, width))
    resid_own, scale_own = resid[:tokens], scale_one[:tokens]
    grad_attn_gain = jnp.sum(d_normed * resid_own * scale_own, axis=0)
    d_block_in = d_mid[:tokens] + norm_backward(d_normed, resid_own, scale_own, attn_gain)
    block_out = (mid[:tokens] + own_summed(down_part)).astype(BF16)

    gains = links.total(
        jnp.concatenate(
            [
                grad_attn_gain,
                grad_mlp_gain,
                jnp.sum(d_q_gain, axis=(0, 1)),
                jnp.sum(d_k_gain, axis=(0, 1)),
            ]
        ).reshape(-1, HEAD_SIZE)
    ).reshape(-1)

    layout = Layout(
        ranks,
        2 * links.chips,
        width,
        grad_gu.shape[1],
        grad_qkv.shape[1],
        grad_down.shape[0],
        grad_out.shape[0],
    )
    parts = ((unit, unit), qkv_units)
    origin = (rank + jnp.arange(ranks, dtype=jnp.int32)) % ranks
    turns = [(core + i) % cores for i in range(cores)]
    shapes = [(a.shape[0], a.shape[1]) for a in (w_gate, w_up, w_query, key_projection)]
    shapes += [value_projection.shape, w_down.shape, w_out.shape]
    whole, waiting, kept = None, [], [[] for _ in range(cores)]

    def take(step, held, numbers):
        nonlocal whole, gains
        if step == 0:
            held[0], gains = lax.optimization_barrier((held[0], gains))
        if whole is not None:
            held, whole = lax.optimization_barrier((held, whole))
        segments, place = [], []
        for value, number in zip(held, numbers):
            for turn in range(cores):
                segments.append(value)
                place += [turns[turn], number, number]
                kept[turn].append((number, value))
                if turn + 1 < cores:
                    value = links.sibling(value)
        waiting.append((segments, place))
        if layout.aligned() and (len(waiting) > 1 or step == links.chips - 1):
            ready, at = waiting.pop(0)
            whole = deliver(layout, parts, cores, ready, places_of(at), shapes, whole)
        return held

    def places_of(at):
        return jnp.concatenate([jnp.stack(at).astype(jnp.int32), origin])

    links.reduce(layout.join(grad_gu, grad_qkv, grad_down, grad_out), layout.spread, take)
    if layout.aligned():
        for ready, at in waiting:
            whole = deliver(layout, parts, cores, ready, places_of(at), shapes, whole)
    else:
        splits = []
        for pairs in kept:
            joined = jnp.zeros((layout.segs, layout.spread + layout.plain, layout.unit), BF16)
            for number, value in pairs:
                joined = lax.dynamic_update_index_in_dim(joined, value, number, 0)
            splits.append(layout.split(joined))
        whole = []
        for index, group in enumerate(parts):
            first = splits[0][index]
            columns = first.shape[2]
            full = jnp.zeros((first.shape[1], ranks * cores * columns), BF16)
            for split, turn in zip(splits, turns):
                for b in range(ranks):
                    column = (origin[b] * cores + turn) * columns
                    full = lax.dynamic_update_slice(full, split[index][b], (0, column))
            whole += split_columns(full, group)
        for index in (2, 3):
            rows = splits[0][index].shape[0]
            full = jnp.zeros((cores * rows, width), BF16)
            for split, turn in zip(splits, turns):
                full = lax.dynamic_update_slice(full, split[index], (turn * rows, 0))
            whole.append(full.astype(F32))
    total_gate, total_up, total_query, total_key, total_value, total_down, total_out = whole
    return (
        block_out,
        d_block_in,
        total_query,
        total_key,
        total_value,
        total_out,
        total_gate,
        total_up,
        total_down,
        gains[:width],
        gains[width : 2 * width],
        gains[2 * width : 2 * width + HEAD_SIZE],
        gains[2 * width + HEAD_SIZE :],
    )


def solution(mesh):
    rows = P(("replica", "fsdp"), None)
    weight = P("fsdp", None)
    in_specs = (
        (rows,)
        + (weight,) * 7
        + (P(),) * 4
        + (P("replica", None), P(("replica", "fsdp")), rows)
    )
    out_specs = (rows, rows) + (weight,) * 7 + (P(),) * 4
    return jax.shard_map(
        functools.partial(shards, Links(mesh)),
        mesh=mesh,
        in_specs=in_specs,
        out_specs=out_specs,
        check_vma=False,
    )
```

```python
import functools

import jax
import jax.numpy as jnp
import numpy as np
from jax import lax
from jax.experimental import pallas as pl
from jax.experimental.pallas import tpu as pltpu
from jax.sharding import PartitionSpec as P

QUERY_HEADS = 16
KEY_VALUE_HEADS = 8
HEAD_SIZE = 128
GROUP = QUERY_HEADS // KEY_VALUE_HEADS

EPS = 1e-06
THETA = 1000000.0
NEG = -1e30


F32 = jnp.float32
BF16 = jnp.bfloat16


def inv_rms(value):
    return lax.rsqrt(jnp.mean(value * value, axis=-1, keepdims=True) + EPS)


def norm_backward(grad, value, scale, gain):
    upstream = grad * gain
    return scale * (
        upstream - value * scale * scale * jnp.mean(upstream * value, axis=-1, keepdims=True)
    )


def dot_nn(left, right):
    return lax.dot_general(left, right, (((1,), (0,)), ((), ())), preferred_element_type=F32)


def dot_nt(left, right):
    return lax.dot_general(left, right, (((1,), (1,)), ((), ())), preferred_element_type=F32)


def dot_tn(left, right, dtype=F32):
    return lax.dot_general(left, right, (((0,), (0,)), ((), ())), preferred_element_type=dtype)


def rope_tables(position_row, width):
    half = width // 2
    freq = jnp.exp(
        -(jnp.arange(half, dtype=F32) * (2.0 / width)) * jnp.log(jnp.float32(THETA))
    )
    angle = position_row.astype(F32)[:, None] * freq[None, :]
    cos, sin = jnp.cos(angle), jnp.sin(angle)
    return jnp.concatenate([cos, cos], axis=-1), jnp.concatenate([-sin, sin], axis=-1)


def _half_turn(value):
    return pltpu.roll(value, HEAD_SIZE // 2, axis=1)


def _rotated(raw, gain, cos, sin):
    scale = inv_rms(raw)
    normed = raw * scale * gain
    return (normed * cos + _half_turn(normed) * sin).astype(BF16), scale


def _probs(q_rot, k_rot, mask):
    scores = dot_nt(q_rot, k_rot) * HEAD_SIZE ** (-0.5)
    scores = jnp.where(mask > 0.5, scores, NEG)
    top = jnp.max(scores, axis=-1, keepdims=True)
    lse = top + jnp.log(jnp.sum(jnp.exp(scores - top), axis=-1, keepdims=True))
    return jnp.exp(scores - lse)


def _head(index):
    return pl.ds(index * HEAD_SIZE, HEAD_SIZE)


def _row_chunks(rows, body):
    chunk = min(rows, 256)
    if rows == chunk:
        body(pl.ds(0, rows))
    else:

        def step(i, carry):
            body(pl.ds(pl.multiple_of(i * chunk, chunk), chunk))
            return carry

        lax.fori_loop(0, rows // chunk, step, 0)


def _columns(offsets, index, size):
    return pl.ds(pl.multiple_of(offsets[index], 128), size)


def _groups(pieces):
    numbers = list(range(len(pieces)))
    return [g for g in (numbers[:1], numbers[1:]) if g]


def _joined(refs):
    values = [r[...] for r in refs]
    return values[0] if len(values) == 1 else jnp.concatenate(values, axis=0)


def _piecewise(left, rows, offsets, pieces):
    total = None
    for group in _groups(pieces):
        parts = [left[rows, _columns(offsets, i, pieces[i].shape[0])] for i in group]
        part = dot_nn(
            parts[0] if len(parts) == 1 else jnp.concatenate(parts, axis=1),
            _joined([pieces[i] for i in group]),
        )
        total = part if total is None else total + part
    return total


def _add_piecewise(out, grad, offsets, pieces):
    for group in _groups(pieces):
        part = dot_nt(grad, _joined([pieces[i] for i in group]))
        start = 0
        for i in group:
            size = pieces[i].shape[0]
            out[:, _columns(offsets, i, size)] += part[:, start : start + size]
            start += size


def attention_kernel(count, offsets, normed, *refs):
    pieces = refs[:count]
    cos, sin, mask, q_gain, k_gain, out, qkv, k_scr, v_scr = refs[count:]

    def project(rows):
        block = _piecewise(normed, rows, offsets, pieces)
        qkv[rows, :] = block
        k_raw = block[:, GROUP * HEAD_SIZE : (GROUP + 1) * HEAD_SIZE]
        k_scr[rows, :], _ = _rotated(k_raw, k_gain[...], cos[rows, :], sin[rows, :])
        v_scr[rows, :] = block[:, (GROUP + 1) * HEAD_SIZE :].astype(BF16)

    def attend(rows):
        for h in range(GROUP):
            q_rot, _ = _rotated(qkv[rows, _head(h)], q_gain[...], cos[rows, :], sin[rows, :])
            probs = _probs(q_rot, k_scr[...], mask[rows, :]).astype(BF16)
            out[rows, _head(h)] = dot_nn(probs, v_scr[...]).astype(BF16)

    _row_chunks(normed.shape[0], project)
    _row_chunks(normed.shape[0], attend)


def attention_back_kernel(
    qkv, cos, sin, mask, q_gain, k_gain, d_attn, d_qkv, d_q_gain, d_k_gain, k_scr, v_scr, dk_scr, dv_scr
):
    total = qkv.shape[0]

    def prepare(rows):
        k_scr[rows, :], _ = _rotated(qkv[rows, _head(GROUP)], k_gain[...], cos[rows, :], sin[rows, :])
        v_scr[rows, :] = qkv[rows, _head(GROUP + 1)].astype(BF16)
        dk_scr[rows, :] = jnp.zeros((rows.size, HEAD_SIZE), F32)
        dv_scr[rows, :] = jnp.zeros((rows.size, HEAD_SIZE), F32)

    def queries(rows):
        for h in range(GROUP):
            q_raw = qkv[rows, _head(h)]
            q_rot, q_scale = _rotated(q_raw, q_gain[...], cos[rows, :], sin[rows, :])
            probs = _probs(q_rot, k_scr[...], mask[rows, :])
            grad = d_attn[rows, _head(h)]
            d_prob = dot_nt(grad, v_scr[...])
            d_scores = (
                probs
                * (d_prob - jnp.sum(probs * d_prob, axis=-1, keepdims=True))
                * HEAD_SIZE ** (-0.5)
            ).astype(BF16)
            d_q = dot_nn(d_scores, k_scr[...])
            dk_scr[...] += dot_tn(d_scores, q_rot)
            dv_scr[...] += dot_tn(probs.astype(BF16), grad)
            d_normed = d_q * cos[rows, :] - _half_turn(d_q) * sin[rows, :]
            d_q_gain[0] += jnp.sum(d_normed * q_raw * q_scale, axis=0, keepdims=True)
            d_qkv[rows, _head(h)] = norm_backward(d_normed, q_raw, q_scale, q_gain[...]).astype(BF16)

    def keys(rows):
        k_raw = qkv[rows, _head(GROUP)]
        k_scale = inv_rms(k_raw)
        d_k = dk_scr[rows, :]
        d_normed = d_k * cos[rows, :] - _half_turn(d_k) * sin[rows, :]
        d_k_gain[0] += jnp.sum(d_normed * k_raw * k_scale, axis=0, keepdims=True)
        d_qkv[rows, _head(GROUP)] = norm_backward(d_normed, k_raw, k_scale, k_gain[...]).astype(BF16)
        d_qkv[rows, _head(GROUP + 1)] = dv_scr[rows, :].astype(BF16)

    d_q_gain[...] = jnp.zeros(d_q_gain.shape, F32)
    d_k_gain[...] = jnp.zeros(d_k_gain.shape, F32)
    _row_chunks(total, prepare)
    _row_chunks(total, queries)
    _row_chunks(total, keys)


def _whole(shape):
    return pl.BlockSpec(shape, lambda *g: (0,) * len(shape))


def attention(normed, pieces, offsets, cos, sin, mask, q_gain, k_gain):
    tokens, _ = normed.shape
    width = pieces[0].shape[1]
    packed = (GROUP + 2) * HEAD_SIZE
    groups = width // packed
    return pl.pallas_call(
        functools.partial(attention_kernel, len(pieces)),
        grid_spec=pltpu.PrefetchScalarGridSpec(
            num_scalar_prefetch=1,
            grid=(groups,),
            in_specs=[
                _whole(normed.shape),
                *[pl.BlockSpec((p.shape[0], packed), lambda g, _: (0, g)) for p in pieces],
                _whole(cos.shape),
                _whole(sin.shape),
                _whole(mask.shape),
                _whole(q_gain.shape),
                _whole(k_gain.shape),
            ],
            out_specs=[
                pl.BlockSpec((tokens, GROUP * HEAD_SIZE), lambda g, _: (0, g)),
                pl.BlockSpec((tokens, packed), lambda g, _: (0, g)),
            ],
            scratch_shapes=[pltpu.VMEM((tokens, HEAD_SIZE), BF16)] * 2,
        ),
        out_shape=[
            jax.ShapeDtypeStruct((tokens, groups * GROUP * HEAD_SIZE), BF16),
            jax.ShapeDtypeStruct((tokens, width), F32),
        ],
        name="attention",
    )(offsets, normed, *pieces, cos, sin, mask, q_gain, k_gain)


def attention_back(qkv, cos, sin, mask, q_gain, k_gain, d_attn):
    tokens, width = qkv.shape
    packed = (GROUP + 2) * HEAD_SIZE
    groups = width // packed
    return pl.pallas_call(
        attention_back_kernel,
        grid=(groups,),
        in_specs=[
            pl.BlockSpec((tokens, packed), lambda g: (0, g)),
            _whole(cos.shape),
            _whole(sin.shape),
            _whole(mask.shape),
            _whole(q_gain.shape),
            _whole(k_gain.shape),
            pl.BlockSpec((tokens, GROUP * HEAD_SIZE), lambda g: (0, g)),
        ],
        out_specs=[
            pl.BlockSpec((tokens, packed), lambda g: (0, g)),
            pl.BlockSpec((1, 1, HEAD_SIZE), lambda g: (g, 0, 0)),
            pl.BlockSpec((1, 1, HEAD_SIZE), lambda g: (g, 0, 0)),
        ],
        out_shape=[
            jax.ShapeDtypeStruct((tokens, width), BF16),
            jax.ShapeDtypeStruct((groups, 1, HEAD_SIZE), F32),
            jax.ShapeDtypeStruct((groups, 1, HEAD_SIZE), F32),
        ],
        scratch_shapes=[pltpu.VMEM((tokens, HEAD_SIZE), BF16)] * 2
        + [pltpu.VMEM((tokens, HEAD_SIZE), F32)] * 2,
        name="attention_back",
    )(qkv, cos, sin, mask, q_gain, k_gain, d_attn)


def mlp_kernel(count, offsets, normed, cotangent, *refs):
    pieces = refs[:count]
    w_down, hidden, d_gu, d_normed, down = refs[count:]
    unit = w_down.shape[0]

    @pl.when(pl.program_id(0) == 0)
    def _():
        d_normed[...] = jnp.zeros(d_normed.shape, F32)
        down[...] = jnp.zeros(down.shape, F32)

    gate_up = _piecewise(normed, slice(None), offsets, pieces)
    gate, up = gate_up[:, :unit], gate_up[:, unit:]
    d_hidden = dot_nt(cotangent[...], w_down[...])
    sig = jax.nn.sigmoid(gate)
    hid = (gate * sig * up).astype(BF16)
    hidden[...] = hid
    d_gu[:, :unit] = (d_hidden * up * sig * (1.0 + gate * (1.0 - sig))).astype(BF16)
    d_gu[:, unit:] = (d_hidden * gate * sig).astype(BF16)
    _add_piecewise(d_normed, d_gu[...], offsets, pieces)
    down[...] += dot_nn(hid, w_down[...])


def mlp(normed, cotangent, pieces, offsets, w_down, unit):
    tokens, width = normed.shape
    ff = w_down.shape[0]
    return pl.pallas_call(
        functools.partial(mlp_kernel, len(pieces)),
        grid_spec=pltpu.PrefetchScalarGridSpec(
            num_scalar_prefetch=1,
            grid=(ff // unit,),
            in_specs=[
                _whole(normed.shape),
                _whole(cotangent.shape),
                *[pl.BlockSpec((p.shape[0], 2 * unit), lambda g, _: (0, g)) for p in pieces],
                pl.BlockSpec((unit, width), lambda g, _: (g, 0)),
            ],
            out_specs=[
                pl.BlockSpec((tokens, unit), lambda g, _: (0, g)),
                pl.BlockSpec((tokens, 2 * unit), lambda g, _: (0, g)),
                _whole((tokens, width)),
                _whole((tokens, width)),
            ],
        ),
        out_shape=[
            jax.ShapeDtypeStruct((tokens, ff), BF16),
            jax.ShapeDtypeStruct((tokens, 2 * ff), BF16),
            jax.ShapeDtypeStruct((tokens, width), F32),
            jax.ShapeDtypeStruct((tokens, width), F32),
        ],
        name="mlp",
    )(offsets, normed, cotangent, *pieces, w_down)


def back_project_kernel(count, offsets, grad, *refs):
    pieces, out = refs[:count], refs[count]

    @pl.when(pl.program_id(0) == 0)
    def _():
        out[...] = jnp.zeros(out.shape, F32)

    _add_piecewise(out, grad[...], offsets, pieces)


def back_project(grad, pieces, offsets, width):
    tokens, wide = grad.shape
    block = min(wide, 1024)
    return pl.pallas_call(
        functools.partial(back_project_kernel, len(pieces)),
        grid_spec=pltpu.PrefetchScalarGridSpec(
            num_scalar_prefetch=1,
            grid=(wide // block,),
            in_specs=[
                pl.BlockSpec((tokens, block), lambda g, _: (0, g)),
                *[pl.BlockSpec((p.shape[0], block), lambda g, _: (0, g)) for p in pieces],
            ],
            out_specs=_whole((tokens, width)),
        ),
        out_shape=jax.ShapeDtypeStruct((tokens, width), F32),
        name="back_project",
    )(offsets, grad, *pieces)


def pack_kernel(units, place_ref, *refs):
    arrays, out = refs[:-1], refs[-1]
    start = 0
    for i in range(arrays[0].shape[1] // units[0]):
        for a, u in zip(arrays, units):
            out[:, start : start + u] = a[:, i * u : (i + 1) * u]
            start += u


def pack(arrays, units, column, count, rows, from_row):
    steps = arrays[0].shape[1] // count // units[0]
    batch = next(b for b in (3, 2, 1) if steps % b == 0)
    place = jnp.stack([column * (steps // batch), from_row]).astype(jnp.int32)
    unit = sum(units)
    return pl.pallas_call(
        functools.partial(pack_kernel, units),
        grid_spec=pltpu.PrefetchScalarGridSpec(
            num_scalar_prefetch=1,
            grid=(steps // batch,),
            in_specs=[
                pl.BlockSpec((rows, batch * u), lambda i, place: (place[1], place[0] + i))
                for u in units
            ],
            out_specs=pl.BlockSpec((rows, batch * unit), lambda i, place: (0, i)),
        ),
        out_shape=jax.ShapeDtypeStruct((rows, steps * unit), BF16),
        name="pack",
    )(place, *arrays)


class Layout:
    def __init__(self, ranks, cores, segs, width, gu, qkv, down_rows, out_rows):
        self.ranks, self.cores, self.segs, self.width = ranks, cores, segs, width
        self.gu, self.qkv = gu, qkv
        self.unit = int(np.gcd.reduce([gu, qkv, width]))
        self.seg = width // ranks // segs
        self.down_seg, self.out_seg = down_rows // segs, out_rows // segs
        self.wide = width // self.unit
        self.down_size, self.out_size = self.down_seg * self.wide, self.out_seg * self.wide
        self.gu_size = ranks * gu // self.unit * self.seg
        self.qkv_size = ranks * qkv // self.unit * self.seg
        self.mlp_size = self.down_size + self.gu_size
        self.size = self.mlp_size + self.qkv_size + self.out_size

    def spread(self, grad):
        units = grad.shape[1] // self.unit
        split = grad.reshape(self.ranks, self.segs, self.seg, units, self.unit)
        return split.transpose(1, 0, 3, 2, 4).reshape(self.segs, -1, self.unit)

    def plain(self, grad):
        split = grad.reshape(self.segs, -1, self.wide, self.unit)
        return split.transpose(0, 2, 1, 3).reshape(self.segs, -1, self.unit)

    def split(self, joined):
        def spread(part):
            part = part.reshape(self.segs, self.ranks, -1, self.seg, self.unit)
            return part.transpose(1, 0, 3, 2, 4).reshape(self.ranks, self.segs * self.seg, -1)

        def plain(part):
            split = part.reshape(self.segs, self.wide, -1, self.unit)
            return split.transpose(0, 2, 1, 3).reshape(-1, self.width)

        cuts = np.cumsum([self.down_size, self.gu_size, self.qkv_size])
        down, gu, qkv, out = jnp.split(joined, cuts, axis=1)
        return spread(gu), spread(qkv), plain(down), plain(out)

    def aligned(self):
        return self.cores == 2 and not (
            self.seg % 16
            or self.down_seg % 16
            or self.out_seg % 16
            or self.unit % 256
            or self.down_size % self.seg
            or self.qkv_size % self.out_seg
        )


def segment_kernel(core_ref, left, left_far, right, right_far, *refs):
    out = refs[-1]
    total = dot_tn(left[...], right[...]) + dot_tn(left_far[...], right_far[...])
    out[...] = total.astype(BF16).reshape(out.shape)


def segment_grads(core, lefts, rights, left_columns, unit, grid, left_at, right_at, out_at, size, segs, before):
    tokens = lefts[0].shape[0]
    rows = left_columns // segs
    aliases = {} if before is None else {5: 0}
    extra = [] if before is None else [before]
    return pl.pallas_call(
        segment_kernel,
        grid_spec=pltpu.PrefetchScalarGridSpec(
            num_scalar_prefetch=1,
            grid=grid,
            in_specs=[pl.BlockSpec((tokens, left_columns), left_at)] * 2
            + [pl.BlockSpec((tokens, unit), right_at)] * 2
            + [pl.BlockSpec(memory_space=pl.ANY)] * len(extra),
            out_specs=pl.BlockSpec((segs, rows, unit), out_at),
        ),
        out_shape=jax.ShapeDtypeStruct((segs, size, unit), BF16),
        input_output_aliases=aliases,
        name="segment_grads",
    )(core, *lefts, *rights, *extra)


def deliver_kernel(layout, parts, cores, count, place, *refs):
    segments = refs[:count]
    tail = refs[-(2 * 7 + 1) :]
    outs, scratch, sems = tail[:7], tail[7:14], tail[14]
    lay = layout
    pending = []
    for k, segment in enumerate(segments):
        core, seg = place[3 * k], place[3 * k + 1]
        row = pl.multiple_of(seg * lay.seg, 16)

        def put(out, buffer, at_row, at_column):
            rows, columns = buffer.shape
            copy = pltpu.make_async_copy(
                buffer,
                out.at[pl.ds(at_row, rows), pl.ds(at_column, columns)],
                sems.at[len(pending)],
            )
            copy.start()
            pending.append(copy)

        def plain(index, rows, start):
            for u in range(lay.wide):
                scratch[index][k, :, u * lay.unit : (u + 1) * lay.unit] = segment[
                    start : start + rows, :
                ].astype(F32)
                start += rows
            at_row = pl.multiple_of((core * lay.segs + seg) * rows, 16)
            put(outs[index], scratch[index].at[k], at_row, 0)

        def spread(index, group, columns, start):
            for b in range(lay.ranks):
                block = place[3 * count + b] * cores + core
                for u in range(columns // lay.unit):
                    value = segment[start : start + lay.seg, :].astype(F32)
                    start += lay.seg
                    left = 0
                    while left < lay.unit:
                        for p, part in enumerate(group):
                            step = u * (lay.unit // sum(group)) + left // sum(group)
                            at = sum(group[:p]) + left
                            scratch[index + p][
                                k * lay.ranks + b, :, step * part : (step + 1) * part
                            ] = value[:, at : at + part]
                        left += sum(group)
                for p in range(len(group)):
                    buffer = scratch[index + p].at[k * lay.ranks + b]
                    at_column = pl.multiple_of(block * buffer.shape[1], 128)
                    put(outs[index + p], buffer, row, at_column)

        plain(5, lay.down_seg, 0)
        spread(0, parts[0], lay.gu, lay.down_size)
        spread(2, parts[1], lay.qkv, lay.mlp_size)
        plain(6, lay.out_seg, lay.mlp_size + lay.qkv_size)
    for copy in pending:
        copy.wait()


def deliver(layout, parts, cores, segments, place, shapes, before):
    count = len(segments)
    lay = layout
    anywhere = pl.BlockSpec(memory_space=pl.ANY)
    widths = [lay.gu // sum(parts[0]) * p for p in parts[0]]
    widths += [lay.qkv // sum(parts[1]) * p for p in parts[1]]
    scratch = [pltpu.VMEM((count * lay.ranks, lay.seg, w), F32) for w in widths]
    scratch += [pltpu.VMEM((count, r, lay.width), F32) for r in (lay.down_seg, lay.out_seg)]
    copies = count * (lay.ranks * len(widths) + 2)
    rows = lay.size
    before = [] if before is None else list(before)
    return pl.pallas_call(
        functools.partial(deliver_kernel, layout, parts, cores, count),
        grid_spec=pltpu.PrefetchScalarGridSpec(
            num_scalar_prefetch=1,
            grid=(1,),
            in_specs=[_whole((rows, lay.unit))] * count + [anywhere] * len(before),
            out_specs=[anywhere] * len(shapes),
            scratch_shapes=scratch + [pltpu.SemaphoreType.DMA((copies,))],
        ),
        out_shape=[jax.ShapeDtypeStruct(shape, F32) for shape in shapes],
        input_output_aliases={1 + count + i: i for i in range(len(before))},
        name="deliver",
    )(place, *segments, *before)


def split_columns(full, parts):
    unit, start, outs = sum(parts), 0, []
    for part in parts:
        pieces = [full[:, i + start : i + start + part] for i in range(0, full.shape[1], unit)]
        outs.append(jnp.concatenate(pieces, axis=1).astype(F32))
        start += part
    return outs


def chip_cycle(mesh):
    column = mesh.devices.reshape(mesh.shape["replica"], mesh.shape["fsdp"])[:, 0]
    total = len(column)
    coords = [tuple(getattr(d, "coords", None) or ()) for d in column]
    cores = 1
    if all(coords):
        while cores < total and coords[cores] == coords[0]:
            cores += 1
    chips = coords[::cores]
    count = len(chips)
    order = list(range(count))
    if count * cores == total and len(set(chips)) == count and all(chips):
        varying = [a for a in range(3) if len({c[a] for c in chips}) > 1]
        if len(varying) == 2:
            values = [sorted({c[a] for c in chips}) for a in varying]
            place = {
                tuple(values[i].index(c[a]) for i, a in enumerate(varying)): k
                for k, c in enumerate(chips)
            }
            high, wide = len(values[0]), len(values[1])
            if high * wide == count:
                if high % 2:
                    place = {(b, a): k for (a, b), k in place.items()}
                    high, wide = wide, high
                if high % 2 == 0:
                    walk = []
                    for row in range(high):
                        cols = range(1, wide) if row % 2 == 0 else range(wide - 1, 0, -1)
                        walk += [(row, col) for col in cols]
                    walk += [(row, 0) for row in range(high - 1, -1, -1)]
                    order = [place[w] for w in walk]
    return cores, order


class Links:
    def __init__(self, mesh):
        self.ranks = mesh.shape["fsdp"]
        self.replicas = mesh.shape["replica"]
        self.cores, self.cycle = chip_cycle(mesh)
        self.chips = len(self.cycle)
        table = np.zeros((self.chips,), np.int32)
        for place, chip in enumerate(self.cycle):
            table[chip] = place
        self.table = table

    def start(self):
        self.rank = lax.axis_index("fsdp")
        replica = lax.axis_index("replica")
        self.core = replica % self.cores
        self.side = (replica // self.cores) % 2
        self.place = jnp.asarray(self.table)[replica // self.cores]

    def from_rank(self, value, shift):
        pairs = [(i, (i - shift) % self.ranks) for i in range(self.ranks)]
        return lax.ppermute(value, "fsdp", pairs)

    def others(self, value):
        return [self.from_rank(value, s) for s in range(1, self.ranks)]

    def sibling(self, value):
        pairs = [
            (chip * self.cores + core, chip * self.cores + (core + 1) % self.cores)
            for chip in range(self.chips)
            for core in range(self.cores)
        ]
        return lax.ppermute(value, "replica", pairs)

    def beside(self, value):
        pairs = [
            (chip * self.cores + core, (chip ^ 1) * self.cores + core)
            for chip in range(self.chips)
            for core in range(self.cores)
        ]
        return lax.ppermute(value, "replica", pairs)

    def along(self, value, direction):
        pairs = [
            (
                self.cycle[i] * self.cores + core,
                self.cycle[(i + direction) % self.chips] * self.cores + core,
            )
            for i in range(self.chips)
            for core in range(self.cores)
        ]
        return lax.ppermute(value, "replica", pairs)

    def total_steps(self):
        steps = []

        def doubled(axis, size, reach):
            pairs = [(i, i ^ reach) for i in range(size)]
            return lambda value: value + lax.ppermute(value, axis, pairs)

        for axis, size in (("replica", self.replicas), ("fsdp", self.ranks)):
            if size & (size - 1):
                steps.append(functools.partial(lax.psum, axis_name=axis))
                continue
            reach = 1
            while reach < size:
                steps.append(doubled(axis, size, reach))
                reach *= 2
        return steps

    def reduce(self, grad, first, spread):
        chips = self.chips

        def local(turn, index):
            return lax.dynamic_index_in_dim(grad, self.segment(turn, index), 0, keepdims=False)

        held = [local(t, q) for t, q in enumerate(self.starts())]
        for step in range(chips - 1):
            for t, direction in enumerate((1, -1)):
                got = self.along(held[t], direction).astype(F32)
                own = local(t, self.starts()[t] - step - 1).astype(F32)
                held[t] = (got + own).astype(BF16)
        return [self.swap(h, first, spread) for h in held]

    def starts(self):
        return [self.place, (self.chips - self.place) % self.chips]

    def segment(self, turn, index):
        return turn * self.chips + lax.rem(index + 2 * self.chips, self.chips)

    def gather(self, held, take):
        for step in range(self.chips):
            numbers = [self.segment(t, q + 1 - step) for t, q in enumerate(self.starts())]
            held = take(step, held, numbers)
            if step < self.chips - 1:
                held = [self.along(h, d) for h, d in zip(held, (1, -1))]

    def swap(self, value, first, spread):
        size = spread // self.ranks

        def block(rank):
            return lax.dynamic_slice_in_dim(value, first + rank * size, size, 0)

        pieces = [value[:first], block(self.rank)]
        for s in range(1, self.ranks):
            pieces.append(self.from_rank(block((self.rank - s + self.ranks) % self.ranks), s))
        return jnp.concatenate(pieces + [value[first + spread :]], axis=0)


def shards(
    links,
    block_in,
    w_query,
    key_projection,
    value_projection,
    w_out,
    w_gate,
    w_up,
    w_down,
    attn_gain,
    mlp_gain,
    query_gain,
    key_norm_gain,
    segment_ids,
    positions,
    cotangent,
):
    links.start()
    ranks, cores = links.ranks, links.cores
    rank, core = links.rank, links.core
    tokens, width = block_in.shape
    sequence = tokens * ranks
    segment_row = segment_ids[0]

    hidden_units = w_down.shape[0]
    unit = 256 if hidden_units % 512 == 0 else 128
    qkv_units = (GROUP * HEAD_SIZE, HEAD_SIZE, HEAD_SIZE)

    def column_block(arrays, units, after):
        rows = arrays[0].shape[0]
        by_cores = cores if rows % (128 * cores) == 0 else 1
        by_chips = 2 if links.chips % 2 == 0 and rows % (256 * by_cores) == 0 else 1
        size = rows // (by_cores * by_chips)
        pieces, places, came = [], [], None
        for s in range(1, ranks):
            to = (rank - s + ranks) % ranks
            mine = (core if by_cores > 1 else 0 * core) * by_chips
            side = links.side if by_chips > 1 else 0 * core
            sent = pack(arrays, units, to, ranks, size, mine + side)
            if after is not None:
                sent, _ = lax.optimization_barrier((sent, after))
            piece = links.from_rank(sent, s)
            came = piece
            base = ((rank + s) % ranks) * rows
            got = [(piece, core, side)]
            if by_chips > 1:
                got.append((links.beside(piece), core, 1 - side))
            for piece, held, at_side in got:
                for turn in range(by_cores):
                    pieces.append(piece)
                    part = (held if by_cores > 1 else 0 * core) * by_chips + at_side
                    places.append(base + part * size)
                    if turn + 1 < by_cores:
                        piece = links.sibling(piece)
                        held = (held - 1 + cores) % cores
        own = pack(arrays, units, rank, ranks, rows, 0 * rank)
        offsets = jnp.stack([rank * rows] + places).astype(jnp.int32)
        return [own] + pieces, offsets, came

    rows_in = jnp.concatenate([block_in] + links.others(block_in), axis=0)
    position_row = jnp.concatenate([positions] + links.others(positions), axis=0)
    w_qkv, at_qkv, came = column_block(
        (w_query, key_projection, value_projection), qkv_units, None
    )
    if came is None:
        came = rows_in
    far_cot, _ = lax.optimization_barrier((cotangent, came[:8, :128]))
    cot = jnp.concatenate([cotangent] + links.others(far_cot), axis=0)
    w_gu, at_gu, _ = column_block((w_gate, w_up), (unit, unit), came[:8, :128])

    offset = rank * tokens
    token = lax.rem(offset + jnp.arange(sequence, dtype=jnp.int32), sequence)
    segments = lax.dynamic_slice_in_dim(
        jnp.concatenate([segment_row, segment_row]), offset, sequence
    )
    mask = (
        (token[None, :] <= token[:, None]) & (segments[None, :] == segments[:, None])
    ).astype(F32)
    cos_tab, sin_tab = rope_tables(position_row, HEAD_SIZE)
    q_gain, k_gain = query_gain[None, :], key_norm_gain[None, :]

    resid = rows_in.astype(F32)
    scale_one = inv_rms(resid)
    normed = (resid * scale_one * attn_gain).astype(BF16)
    attn_out, qkv = attention(normed, w_qkv, at_qkv, cos_tab, sin_tab, mask, q_gain, k_gain)
    mid_part = dot_nn(attn_out, w_out)

    def all_summed(part):
        total = part
        sent = part.astype(BF16)
        for s in range(1, ranks):
            got = links.from_rank(sent, s)
            total = total + jnp.roll(got, s * tokens, axis=0).astype(F32)
        return total

    def own_summed(part):
        total = part[:tokens]
        for s in range(1, ranks):
            far = (ranks - s) * tokens
            total = total + links.from_rank(part[far : far + tokens].astype(BF16), s).astype(F32)
        return total

    mid = resid + all_summed(mid_part)
    scale_two = inv_rms(mid)
    normed_two = (mid * scale_two * mlp_gain).astype(BF16)
    hidden, d_gu, d_normed_part, down_part = mlp(normed_two, cot, w_gu, at_gu, w_down, unit)

    d_normed_two = all_summed(d_normed_part)

    def both(value):
        return jnp.concatenate([value, links.sibling(value)], axis=0) if cores > 1 else value

    def both_of_columns(value):
        size = value.shape[1] // cores
        own = lax.dynamic_slice_in_dim(value, core * size, size, 1)
        if cores == 1:
            return own
        theirs = lax.dynamic_slice_in_dim(value, ((core + 1) % cores) * size, size, 1)
        return jnp.concatenate([own, links.sibling(theirs)], axis=0)

    gu_width, qkv_width = d_gu.shape[1] // cores, w_qkv[0].shape[1] // cores
    layout = Layout(
        ranks,
        cores,
        2 * links.chips,
        width,
        gu_width,
        qkv_width,
        hidden_units // cores,
        w_out.shape[0] // cores,
    )
    core_at = jnp.reshape(core, (1,)).astype(jnp.int32)
    lay = layout

    def spread_grads(left, right, columns, first, size, before):
        units = columns // lay.unit
        return segment_grads(
            core_at,
            [left, links.sibling(left)],
            [right, links.sibling(right)],
            width // ranks,
            lay.unit,
            (ranks, units),
            lambda b, u, c: (0, b),
            lambda b, u, c: (0, c[0] * units + u),
            lambda b, u, c: (0, first // lay.seg + b * units + u, 0),
            size,
            lay.segs,
            before,
        )

    def plain_grads(left, right, first, size, before):
        columns = left.shape[1] // cores
        return segment_grads(
            core_at,
            [left, links.sibling(left)],
            [right, links.sibling(right)],
            columns,
            lay.unit,
            (lay.wide,),
            lambda u, c: (0, c[0]),
            lambda u, c: (0, u),
            lambda u, c: (0, first // (columns // lay.segs) + u, 0),
            size,
            lay.segs,
            before,
        )

    if layout.aligned():
        mlp_grads = spread_grads(normed_two, d_gu, gu_width, lay.down_size, lay.mlp_size, None)
        mlp_grads = plain_grads(hidden, cot, 0, lay.mlp_size, mlp_grads)
    else:
        grad_gu = dot_tn(both(normed_two), both_of_columns(d_gu), BF16)
        grad_down = dot_tn(both_of_columns(hidden), both(cot), BF16)
        mlp_grads = jnp.concatenate([lay.plain(grad_down), lay.spread(grad_gu)], axis=1)
    mlp_held = links.reduce(mlp_grads, lay.down_size, lay.gu_size)

    grad_mlp_gain = jnp.sum((d_normed_two * mid * scale_two)[:tokens], axis=0)
    d_mid = cot.astype(F32) + norm_backward(d_normed_two, mid, scale_two, mlp_gain)
    d_mid_b = d_mid.astype(BF16)
    d_attn = dot_nt(d_mid_b, w_out).astype(BF16)
    d_qkv, d_q_gain, d_k_gain = attention_back(
        qkv, cos_tab, sin_tab, mask, q_gain, k_gain, d_attn
    )
    attn_size = lay.qkv_size + lay.out_size
    if layout.aligned():
        attn_grads = plain_grads(attn_out, d_mid_b, lay.qkv_size, attn_size, None)
        attn_grads = spread_grads(normed, d_qkv, qkv_width, 0, attn_size, attn_grads)
    else:
        grad_qkv = dot_tn(both(normed), both_of_columns(d_qkv), BF16)
        grad_out = dot_tn(both_of_columns(attn_out), both(d_mid_b), BF16)
        attn_grads = jnp.concatenate([lay.spread(grad_qkv), lay.plain(grad_out)], axis=1)
    attn_held = links.reduce(attn_grads, 0, lay.qkv_size)

    d_normed = own_summed(back_project(d_qkv, w_qkv, at_qkv, width))
    resid_own, scale_own = resid[:tokens], scale_one[:tokens]
    grad_attn_gain = jnp.sum(d_normed * resid_own * scale_own, axis=0)
    d_block_in = d_mid[:tokens] + norm_backward(d_normed, resid_own, scale_own, attn_gain)
    block_out = (mid[:tokens] + own_summed(down_part)).astype(BF16)

    gains = jnp.concatenate(
        [
            grad_attn_gain,
            grad_mlp_gain,
            jnp.sum(d_q_gain, axis=(0, 1)),
            jnp.sum(d_k_gain, axis=(0, 1)),
        ]
    ).reshape(-1, HEAD_SIZE)
    gain_steps = links.total_steps()

    parts = ((unit, unit), qkv_units)
    origin = (rank + jnp.arange(ranks, dtype=jnp.int32)) % ranks
    turns = [(core + i) % cores for i in range(cores)]
    shapes = [(a.shape[0], a.shape[1]) for a in (w_gate, w_up, w_query, key_projection)]
    shapes += [value_projection.shape, w_down.shape, w_out.shape]
    whole, waiting, kept = None, [], [[] for _ in range(cores)]

    def take(step, held, numbers):
        nonlocal whole, gains
        if gain_steps:
            held[0], gains = lax.optimization_barrier((held[0], gains))
            gains = gain_steps.pop(0)(gains)
        if whole is not None:
            held, whole = lax.optimization_barrier((held, whole))
        segments, place = [], []
        for value, number in zip(held, numbers):
            for turn in range(cores):
                segments.append(value)
                place += [turns[turn], number, number]
                kept[turn].append((number, value))
                if turn + 1 < cores:
                    value = links.sibling(value)
        waiting.append((segments, place))
        if layout.aligned() and (len(waiting) > 1 or step == links.chips - 1):
            ready, at = waiting.pop(0)
            whole = deliver(layout, parts, cores, ready, places_of(at), shapes, whole)
        return held

    def places_of(at):
        return jnp.concatenate([jnp.stack(at).astype(jnp.int32), origin])

    held = [jnp.concatenate(pair, axis=0) for pair in zip(mlp_held, attn_held)]
    links.gather(held, take)
    for one in gain_steps:
        gains = one(gains)
    gains = gains.reshape(-1)
    if layout.aligned():
        for ready, at in waiting:
            whole = deliver(layout, parts, cores, ready, places_of(at), shapes, whole)
    else:
        splits = []
        for pairs in kept:
            joined = jnp.zeros((layout.segs, layout.size, layout.unit), BF16)
            for number, value in pairs:
                joined = lax.dynamic_update_index_in_dim(joined, value, number, 0)
            splits.append(layout.split(joined))
        whole = []
        for index, group in enumerate(parts):
            first = splits[0][index]
            columns = first.shape[2]
            full = jnp.zeros((first.shape[1], ranks * cores * columns), BF16)
            for split, turn in zip(splits, turns):
                for b in range(ranks):
                    column = (origin[b] * cores + turn) * columns
                    full = lax.dynamic_update_slice(full, split[index][b], (0, column))
            whole += split_columns(full, group)
        for index in (2, 3):
            rows = splits[0][index].shape[0]
            full = jnp.zeros((cores * rows, width), BF16)
            for split, turn in zip(splits, turns):
                full = lax.dynamic_update_slice(full, split[index], (turn * rows, 0))
            whole.append(full.astype(F32))
    total_gate, total_up, total_query, total_key, total_value, total_down, total_out = whole
    return (
        block_out,
        d_block_in,
        total_query,
        total_key,
        total_value,
        total_out,
        total_gate,
        total_up,
        total_down,
        gains[:width],
        gains[width : 2 * width],
        gains[2 * width : 2 * width + HEAD_SIZE],
        gains[2 * width + HEAD_SIZE :],
    )


def solution(mesh):
    rows = P(("replica", "fsdp"), None)
    weight = P("fsdp", None)
    in_specs = (
        (rows,)
        + (weight,) * 7
        + (P(),) * 4
        + (P("replica", None), P(("replica", "fsdp")), rows)
    )
    out_specs = (rows, rows) + (weight,) * 7 + (P(),) * 4
    return jax.shard_map(
        functools.partial(shards, Links(mesh)),
        mesh=mesh,
        in_specs=in_specs,
        out_specs=out_specs,
        check_vma=False,
    )
```
